32 devices in a mesh: pre: 4 (over x, core), dec: 8 (over z, y).
Axes of the slice: x: 2, y: 2, z: 4, core: 2. Of those that a mesh axis runs over, the one named last changes fastest.
Arguments:
- queries: bfloat16 [16, 128, 8192], P('pre', None, 'dec'), may hold values from -6 to 6, as said below
- branch_kv: bfloat16 [16, 128, 2048], P('pre', None, 'dec'), may hold values from -6 to 6
- pool_kv: bfloat16 [16, 128, 2048], P('pre', None, 'dec'), may hold values from -6 to 6, as said below
- page_lists: int32 [16, 16], replicated, may hold values from 0 to 15, as said below
- anc_len: int32 [16], replicated, may hold values from 1025 to 2048
- dec_owner: int32 [16], replicated, may hold values from 0 to 7, as said below
- output_projection_weight: bfloat16 [8192, 8192], P('dec'), may hold values from -0.0625 to 0.0625
Outputs:
- layer_out: bfloat16 [16, 128, 8192], P('pre', None, 'dec')
- decode_pages: bfloat16 [32, 128, 2048], P('dec', None, 'pre')
The draws below stay inside these ranges and needn't reach their ends.
Inputs may be any that keep to these rules, and one draw needn't show every extreme that they name: `queries`: floats within the range. `pool_kv`: floats within the range. `page_lists`: each branch lists distinct pages; the first half of the slots holds the same pages for every branch. `dec_owner`: the 4 branches of one prefill device (branches p * 4 on) go to distinct decode owners; one decode owner receives a branch from every prefill device.
All inputs are finite; a program needn't handle non-finite values.
Results may differ from the reference program's by a relative error of at most 0.024.
Values may be sent and summed in bfloat16 or wider, within the bound.
A program may use at most 128 MiB of HBM per device.

```python
import jax
import jax.numpy as jnp
from jax import lax

D = 8192
QH = 64
KVH = 8
HD = 128
PAGE = 128
NANC = 16
BR_DEV = 4
BRANCHES = 16
NPAGES = 16
N_PRE = 4
N_DEC = 8


def draw_queries(key, part):
    own_key = jax.random.fold_in(key, 11)
    shape = (BRANCHES, PAGE, QH, HD)
    base = jnp.clip(jax.random.normal(own_key, shape, jnp.float32), -6.0, 6.0)
    return base.reshape(BRANCHES, PAGE, QH * HD).astype(jnp.bfloat16)


def draw_pool_kv(key, part):
    own_key = jax.random.fold_in(key, 12)
    shape = (NPAGES, PAGE, KVH, 2, HD)
    base = jnp.clip(jax.random.normal(own_key, shape, jnp.float32), -6.0, 6.0)
    return base.reshape(NPAGES, PAGE, 2 * KVH * HD).astype(jnp.bfloat16)


def draw_page_lists(key, part):
    base_key = jax.random.fold_in(key, 13)
    order = jax.random.permutation(base_key, NPAGES).astype(jnp.int32)
    shared = NANC // 2
    root = order[:shared]
    rest = order[shared:]
    branch_keys = jax.random.split(jax.random.fold_in(base_key, 1), BRANCHES)
    tails = jax.vmap(lambda k: jax.random.permutation(k, rest)[:NANC - shared])(branch_keys)
    heads = jnp.broadcast_to(root[None, :], (BRANCHES, shared))
    return jnp.concatenate([heads, tails], 1).astype(jnp.int32)


def draw_dec_owner(key, part):
    base_key = jax.random.fold_in(key, 14)
    hot = jax.random.randint(base_key, (), 0, N_DEC).astype(jnp.int32)
    row_keys = jax.random.split(jax.random.fold_in(base_key, 1), N_PRE)

    def one_row(row_key):
        first, second = jax.random.split(row_key)
        others = jax.random.permutation(first, N_DEC - 1).astype(jnp.int32)
        others = others + (others >= hot).astype(jnp.int32)
        chosen = jnp.concatenate([hot[None], others[:BR_DEV - 1]])
        return jax.random.permutation(second, chosen)
    return jax.vmap(one_row)(row_keys).reshape(BRANCHES).astype(jnp.int32)


def place_ends(values, rng, least, high):
    longest = values.shape.index(max(values.shape))
    spots = []
    for shift in (0, 1):
        where = [jax.random.randint(jax.random.fold_in(rng, axis), (), 0, length) for axis, length in enumerate(values.shape)]
        where[longest] = (where[longest] + shift) % values.shape[longest]
        spots.append(tuple(where))
    return values.at[spots[0]].set(least).at[spots[1]].set(high)


def steps_of(key, shape, pieces, least, high):
    def one(dim, parts):
        steps = jax.random.uniform(jax.random.fold_in(jax.random.fold_in(key, 6), dim), (parts,), jnp.float32, least / len(pieces), high / len(pieces))
        return jnp.repeat(jnp.exp(steps), shape[dim] // parts).reshape((-1,) + (1,) * (len(shape) - dim - 1))

    gain = one(*pieces[0])
    for cut in pieces[1:]:
        gain = gain * one(*cut)
    return gain


def gaussian(key, extent, deviation, limit, cuts=(), held_as=jnp.bfloat16):
    values = jax.random.normal(key, extent, jnp.float32) * deviation
    if len(cuts) > 0:
        values = steps_of(key, extent, cuts, -0.22, 0.18) * values
    return jnp.clip(values, min=-limit, max=limit).astype(held_as)


def setup_inputs(seed: int = 0) -> dict:
    seeds = jax.random.split(jax.random.key(seed), 8)
    queries = draw_queries(jax.random.fold_in(seeds[7], 71), 0)
    branch_kv = gaussian(seeds[1], (BRANCHES, PAGE, 2 * KVH * HD), 1.0, 6.0, ((0, 4), (2, 8)))
    pool_kv = draw_pool_kv(jax.random.fold_in(seeds[7], 71), 0)
    page_lists = draw_page_lists(jax.random.fold_in(seeds[7], 71), 0)
    anc_len = place_ends(jax.random.randint(seeds[4], (BRANCHES,), NANC // 2 * PAGE + 1, NANC * PAGE + 1), jax.random.fold_in(seeds[4], 1), NANC // 2 * PAGE + 1, NANC * PAGE).astype(jnp.int32)
    dec_owner = draw_dec_owner(jax.random.fold_in(seeds[7], 71), 0)
    output_projection_weight = gaussian(seeds[6], (QH * HD, D), (QH * HD) ** -0.5, 0.0625, ((0, 8),))
    return dict(queries=queries, branch_kv=branch_kv, pool_kv=pool_kv, page_lists=page_lists, anc_len=anc_len, dec_owner=dec_owner, output_projection_weight=output_projection_weight)


def reference(queries, branch_kv, pool_kv, page_lists, anc_len, dec_owner, output_projection_weight):
    group = QH // KVH
    softmax_scale = HD ** -0.5

    def one_branch(item):
        q_rows, own_rows, pages, count = item
        query_vectors = q_rows.reshape(PAGE, QH, HD).astype(jnp.float32)
        ancestors = pool_kv[pages.astype(jnp.int32)].reshape(NANC * PAGE, KVH, 2, HD)
        own = own_rows.reshape(PAGE, KVH, 2, HD)
        keys = jnp.concatenate([ancestors[:, :, 0], own[:, :, 0]], 0)
        values = jnp.concatenate([ancestors[:, :, 1], own[:, :, 1]], 0)
        keys = jnp.repeat(keys, group, axis=1).astype(jnp.float32)
        values = jnp.repeat(values, group, axis=1).astype(jnp.float32)
        scores = jnp.einsum("qhd,khd->qhk", query_vectors, keys) * softmax_scale
        position = jnp.arange(NANC * PAGE, dtype=jnp.int32)
        earlier = jnp.broadcast_to((position < count)[None, :], (PAGE, NANC * PAGE))
        causal = jnp.arange(PAGE, dtype=jnp.int32)[None, :] <= jnp.arange(PAGE, dtype=jnp.int32)[:, None]
        allowed = jnp.concatenate([earlier, causal], 1)
        scores = jnp.where(allowed[:, None, :], scores, -jnp.inf)
        top = jnp.max(scores, axis=-1, keepdims=True)
        weights = jnp.exp(scores - top)
        running_denominator = jnp.sum(weights, axis=-1)
        probs = lax.optimization_barrier(weights.astype(jnp.bfloat16)).astype(jnp.float32)
        out = jnp.einsum("qhk,khd->qhd", probs, values) / running_denominator[..., None]
        return out.reshape(PAGE, QH * HD).astype(jnp.bfloat16)

    attention_result = lax.map(one_branch, (queries, branch_kv, page_lists, anc_len))
    attn_flat = attention_result.reshape(BRANCHES * PAGE, QH * HD)
    width = QH * HD // N_DEC

    def add_group(index, running_denominator):
        start = (index * width).astype(jnp.int32)
        cols = lax.dynamic_slice_in_dim(attn_flat, start, width, 1)
        rows = lax.dynamic_slice_in_dim(output_projection_weight, start, width, 0)
        exponent_term = jnp.dot(cols, rows, preferred_element_type=jnp.float32)
        exponent_term = lax.optimization_barrier(exponent_term.astype(jnp.bfloat16)).astype(jnp.float32)
        return running_denominator + exponent_term

    summed = lax.fori_loop(0, N_DEC, add_group, jnp.zeros((BRANCHES * PAGE, D), jnp.float32))
    layer_out = summed.astype(jnp.bfloat16).reshape(BRANCHES, PAGE, D)

    owners = dec_owner.reshape(N_PRE, BR_DEV)
    onehot = (owners[:, :, None] == jnp.arange(N_DEC, dtype=jnp.int32)[None, None, :]).astype(jnp.float32)
    kv_rows = branch_kv.reshape(N_PRE, BR_DEV, PAGE, 2 * KVH * HD).astype(jnp.float32)
    placed = jnp.einsum("pbo,pbqc->opqc", onehot, kv_rows)
    decode_pages = placed.reshape(N_DEC * N_PRE, PAGE, 2 * KVH * HD).astype(jnp.bfloat16)
    return layer_out, decode_pages
```

```python
import functools
import math

import jax
import jax.numpy as jnp
from jax import lax
from jax.experimental import pallas as pl
from jax.experimental.pallas import tpu as pltpu
from jax.sharding import PartitionSpec as P

HD = 128
MASKED = -1e30
SCALE = HD**-0.5 * math.log2(math.e)
MESH = pl.DeviceIdType.MESH
VMEM = pl.BlockSpec(memory_space=pltpu.VMEM)
SMEM = pl.BlockSpec(memory_space=pltpu.SMEM)
PAIR = 2
WPIECES = 4
CHUNKS = 2


def from_partner(value, axis, stride):
    mask = 2**stride
    pairs = [(source, source ^ mask) for source in range(lax.axis_size(axis))]
    return lax.ppermute(value, axis, pairs)


def load_values(pool_ref, values):
    pages, page_len, _ = pool_ref.shape
    values[:, :HD] = pool_ref[:, :, HD:].reshape(pages * page_len, HD)
    values[:, HD:] = jnp.ones((pages * page_len, HD), values.dtype)


def attend(branch, first, last, q_ref, own_ref, pool_ref, bias_ref, values, attn, after):
    pages, page_len, _ = pool_ref.shape
    keys = pool_ref[:, :, :HD].reshape(pages * page_len, HD)
    own_keys = own_ref[branch, :, :HD]
    own_values = own_ref[branch, :, HD:]
    own_values = jnp.concatenate([own_values, jnp.ones_like(own_values)], 1)
    row = lax.broadcasted_iota(jnp.int32, (page_len, page_len), 0)
    col = lax.broadcasted_iota(jnp.int32, (page_len, page_len), 1)
    causal = jnp.where(col <= row, 0.0, MASKED)
    causal = jnp.concatenate([causal] * PAIR, 0)
    bias = bias_ref[branch]
    nt = (((1,), (1,)), ((), ()))

    def group(g, carry):
        start = pl.multiple_of(g * PAIR * HD, PAIR * HD)
        q = q_ref[branch, :, pl.ds(start, PAIR * HD)]
        q = jnp.concatenate([q[:, i * HD : (i + 1) * HD] for i in range(PAIR)], 0)
        far = lax.dot_general(q, keys, nt, preferred_element_type=jnp.float32) + bias
        near = lax.dot_general(q, own_keys, nt, preferred_element_type=jnp.float32) + causal
        top = jnp.maximum(
            jnp.max(far, axis=-1, keepdims=True), jnp.max(near, axis=-1, keepdims=True)
        )
        top = top * SCALE
        far = jnp.exp2(far * SCALE - top).astype(jnp.bfloat16)
        near = jnp.exp2(near * SCALE - top).astype(jnp.bfloat16)
        out = jnp.dot(far, values[...], preferred_element_type=jnp.float32)
        out = out + jnp.dot(near, own_values, preferred_element_type=jnp.float32)
        out = (out[:, :HD] / out[:, HD:]).astype(jnp.bfloat16)
        for i in range(PAIR):
            attn[branch, :, pl.ds(start + i * HD, HD)] = out[i * page_len : (i + 1) * page_len]
        after(branch, g)
        return carry

    lax.fori_loop(first, last, group, 0)


def layer_kernel(
    n_pre,
    n_dec,
    lists_ref,
    reach_ref,
    owner_ref,
    kv_ref,
    pool_ref,
    q_hbm,
    own_hbm,
    w_ref,
    out_ref,
    pages_ref,
    all_ref,
    q_ref,
    own_ref,
    values,
    attn,
    wv,
    sent,
    got,
    bias_ref,
    bucket_ref,
    row_ref,
    block_ref,
    load_sem,
    wsem,
    psend,
    precv,
    bsend,
    brecv,
    msend,
    mrecv,
    hsend,
    hrecv,
    asend,
    arecv,
    ysend,
    yrecv,
    xsend,
    xrecv,
    csend,
    crecv,
    ssem,
    rsem,
):
    pre = lax.axis_index("pre")
    dec = lax.axis_index("dec")
    branches, page_len, cols = out_ref.shape
    depth = w_ref.shape[0]
    count = pool_ref.shape[0]
    width = kv_ref.shape[2]
    ratio = n_dec // n_pre
    chips = n_pre // 2
    chip = pre // 2
    core = lax.rem(pre, 2)
    spots = n_dec // 2
    spot = dec // 2
    side = lax.rem(dec, 2)
    mate = dec + 1 - 2 * side
    share = depth // n_pre
    pieces = WPIECES
    piece = cols // pieces
    halves = CHUNKS
    half = cols // halves
    per_half = pieces // halves
    groups = depth // (PAIR * HD)
    low = 2 * spot < spots

    def target(step):
        outer = spots - 1 - spot
        rising = jnp.where(step < outer, spots - 1 - step, step - outer)
        falling = jnp.where(step < spot, step, spots - 1 - step + spot)
        return jnp.where(low, rising, falling)

    def block_of(device):
        return pl.ds(device * count, count)

    def across(k):
        return pltpu.make_async_remote_copy(
            src_ref=pool_ref,
            dst_ref=all_ref.at[block_of(pre)],
            send_sem=psend.at[k],
            recv_sem=precv.at[k],
            device_id={"pre": lax.rem(chip + k, chips) * 2 + core},
            device_id_type=MESH,
        )

    def beside(k):
        where = all_ref.at[block_of(lax.rem(chip + chips - k, chips) * 2 + core)]
        return pltpu.make_async_remote_copy(
            src_ref=pool_ref if k == 0 else where,
            dst_ref=where,
            send_sem=psend.at[chips + k],
            recv_sem=precv.at[chips + k],
            device_id={"pre": chip * 2 + 1 - core},
            device_id_type=MESH,
        )

    def own_rows(step):
        t = target(step)
        start = pl.multiple_of((2 * t + side) * cols, cols)
        return pltpu.make_async_copy(
            w_ref.at[:, pl.ds(start, cols)], wv.at[t, pl.ds(0, depth)], wsem.at[step]
        )

    def share_of(device, step, c):
        rows = pl.ds(pl.multiple_of(depth + device * share, 16), share)
        return wv.at[target(step), rows, pl.ds(pl.multiple_of(c * piece, piece), piece)]

    def to_mate(step, c):
        start = pl.multiple_of((2 * target(step) + 1 - side) * cols + c * piece, piece)
        rows = pl.ds(pl.multiple_of(pre * share, 16), share)
        return pltpu.make_async_remote_copy(
            src_ref=w_ref.at[rows, pl.ds(start, piece)],
            dst_ref=share_of(pre, step, c),
            send_sem=ysend.at[step, c],
            recv_sem=yrecv.at[step, c],
            device_id={"dec": mate},
            device_id_type=MESH,
        )

    def to_chip(step, c, k):
        return pltpu.make_async_remote_copy(
            src_ref=share_of(pre, step, c),
            dst_ref=share_of(pre, step, c),
            send_sem=xsend.at[step, c, k],
            recv_sem=xrecv.at[step, c, k],
            device_id={"pre": lax.rem(chip + k, chips) * 2 + core},
            device_id_type=MESH,
        )

    def to_core(step, c, k):
        where = share_of(lax.rem(chip + chips - k, chips) * 2 + core, step, c)
        return pltpu.make_async_remote_copy(
            src_ref=where,
            dst_ref=where,
            send_sem=csend.at[step, c, k],
            recv_sem=crecv.at[step, c, k],
            device_id={"pre": chip * 2 + 1 - core},
            device_id_type=MESH,
        )

    def pass_on(step, c):
        to_mate(step, c).wait_recv()
        for k in range(1, chips):
            to_chip(step, c, k).start()
        to_core(step, c, 0).start()

    def pass_over(step, c):
        for k in range(1, chips):
            to_chip(step, c, k).wait_recv()
            to_core(step, c, k).start()

    def need(step, c):
        for k in range(chips):
            to_core(step, c, k).wait_recv()

    def attn_copy(b, g):
        start = pl.multiple_of(g * PAIR * HD, PAIR * HD)
        return pltpu.make_async_remote_copy(
            src_ref=attn.at[b, :, pl.ds(start, PAIR * HD)],
            dst_ref=attn.at[b, :, pl.ds(depth + start, PAIR * HD)],
            send_sem=asend.at[b, g],
            recv_sem=arecv.at[b, g],
            device_id={"dec": mate},
            device_id_type=MESH,
        )

    def at_half(c):
        return pl.ds(pl.multiple_of(c * half, half), half)

    def arrival(slot, b, c):
        where = got.at[slot, b, :, at_half(c)]
        return pltpu.make_async_copy(where, where, rsem.at[slot, b, c])

    def chunk_copy(step, b, c):
        t = target(step)
        onward = t > spot
        slot = jnp.where(t == spot - 1, spots, t)
        return pltpu.make_async_remote_copy(
            src_ref=sent.at[t, b, :, at_half(c)],
            dst_ref=got.at[slot, b, :, at_half(c)],
            send_sem=ssem.at[step, b, c],
            recv_sem=rsem.at[slot, b, c],
            device_id={"dec": jnp.where(onward, dec + 2, dec - 2)},
            device_id_type=MESH,
        )

    def send_chunk(step, b, c):
        t = target(step)
        relayed = jnp.where(t > spot, spot > 0, spot < spots - 1)

        @pl.when(relayed)
        def _():
            arrival(t, b, c).wait()

        total = jnp.dot(attn[b], wv[t, :, at_half(c)], preferred_element_type=jnp.float32)
        total = total + got[t, b, :, at_half(c)].astype(jnp.float32)
        sent[t, b, :, at_half(c)] = total.astype(jnp.bfloat16)
        chunk_copy(step, b, c).start()

    def last_chunk(b, c):
        @pl.when(spot > 0)
        def _():
            arrival(spot, b, c).wait()

        @pl.when(spot < spots - 1)
        def _():
            arrival(spots, b, c).wait()

        total = jnp.dot(attn[b], wv[spot, :, at_half(c)], preferred_element_type=jnp.float32)
        total = total + got[spot, b, :, at_half(c)].astype(jnp.float32)
        total = total + got[spots, b, :, at_half(c)].astype(jnp.float32)
        out_ref[b, :, at_half(c)] = total.astype(jnp.bfloat16)

    def to_row(k):
        where = lax.rem(spot + k, spots)
        return pltpu.make_async_remote_copy(
            src_ref=bucket_ref.at[where],
            dst_ref=row_ref.at[spot],
            send_sem=bsend.at[k],
            recv_sem=brecv.at[k],
            device_id={"dec": 2 * where + side},
            device_id_type=MESH,
        )

    row_local = pltpu.make_async_copy(bucket_ref.at[spot], row_ref.at[spot], brecv.at[0])
    to_side = pltpu.make_async_remote_copy(
        src_ref=row_ref.at[:, 1 - side],
        dst_ref=block_ref.at[side],
        send_sem=msend.at[0],
        recv_sem=mrecv.at[0],
        device_id={"dec": mate},
        device_id_type=MESH,
    )
    side_local = pltpu.make_async_copy(row_ref.at[:, side], block_ref.at[side], mrecv.at[1])

    def home_parts(k, part):
        home = lax.rem(pre + k, n_pre)
        source = home * ratio + part
        src = block_ref.at[lax.rem(source, 2), source // 2]
        return home, src, pages_ref.at[pre, :, pl.ds(part * width, width)]

    def to_home(k, part):
        home, src, dst = home_parts(k, part)
        return pltpu.make_async_remote_copy(
            src_ref=src,
            dst_ref=dst,
            send_sem=hsend.at[k, part],
            recv_sem=hrecv.at[k, part],
            device_id={"pre": home},
            device_id_type=MESH,
        )

    def home_local(part):
        _, src, dst = home_parts(0, part)
        return pltpu.make_async_copy(src, dst, hrecv.at[0, part])

    def pages_to_side():
        for k in range(1, spots):
            to_row(k).wait_recv()
        row_local.wait()
        to_side.start()
        side_local.start()

    def pages_to_home():
        to_side.wait_recv()
        side_local.wait()
        for part in range(ratio):
            home_local(part).start()
            for k in range(1, n_pre):
                to_home(k, part).start()

    barrier = pltpu.get_barrier_semaphore()
    for k in range(1, n_pre):
        pl.semaphore_signal(
            barrier, 1, device_id={"pre": lax.rem(pre + k, n_pre)}, device_id_type=MESH
        )
    pl.semaphore_signal(barrier, 1, device_id={"dec": mate}, device_id_type=MESH)
    for k in range(1, spots):
        pl.semaphore_signal(
            barrier,
            1,
            device_id={"dec": 2 * lax.rem(spot + k, spots) + side},
            device_id_type=MESH,
        )
    loads = [
        pltpu.make_async_copy(pool_ref, all_ref.at[block_of(pre)], load_sem.at[0]),
        pltpu.make_async_copy(q_hbm, q_ref, load_sem.at[1]),
        pltpu.make_async_copy(own_hbm, own_ref, load_sem.at[2]),
    ]
    for copy in loads:
        copy.start()
    own_rows(0).start()
    pl.semaphore_wait(barrier, n_pre + spots - 1)

    for k in range(1, chips):
        across(k).start()
    beside(0).start()
    for c in range(pieces):
        to_mate(0, c).start()
    first = pre * branches
    for o in range(n_dec):
        bucket = jnp.zeros(kv_ref.shape[1:], kv_ref.dtype)
        for b in range(branches):
            bucket = jnp.where(owner_ref[first + b] == o, kv_ref[b], bucket)
        bucket_ref[o // 2, o % 2] = bucket
    for k in range(1, spots):
        to_row(k).start()
    row_local.start()

    def mask(b, carry):
        visible = jnp.zeros((count * n_pre, page_len), jnp.int32)
        page = lax.broadcasted_iota(jnp.int32, visible.shape, 0)
        token = lax.broadcasted_iota(jnp.int32, visible.shape, 1)
        for slot in range(lists_ref.shape[1]):
            shown = reach_ref[first + b] - slot * page_len
            visible = jnp.where(page == lists_ref[first + b, slot], shown, visible)
        bias = jnp.where(token < visible, 0.0, MASKED).astype(jnp.float32)
        for p in range(count * n_pre):
            bias_ref[b, :, p * page_len : (p + 1) * page_len] = bias[p : p + 1]
        return carry

    lax.fori_loop(0, branches, mask, 0)

    @pl.when(spot == 0)
    def _():
        def clear(t, carry):
            got[t] = jnp.zeros(got.shape[1:], got.dtype)
            return carry

        lax.fori_loop(0, spots, clear, 0)

    @pl.when(spot == spots - 1)
    def _():
        def clear(t, carry):
            got[t + t // (spots - 1)] = jnp.zeros(got.shape[1:], got.dtype)
            return carry

        lax.fori_loop(0, spots, clear, 0)

    for k in range(1, chips):
        across(k).wait_recv()
        beside(k).start()

    for c in range(pieces // 2):
        pass_on(0, c)
    for copy in loads:
        copy.wait()
    for k in range(chips):
        beside(k).wait_recv()
    load_values(all_ref, values)

    def load_rest(step, carry):
        own_rows(step).start()
        return carry

    lax.fori_loop(1, spots, load_rest, 0)

    def after(b, g):
        attn_copy(b, g).start()

    def some(i, first, last):
        @pl.when(i < branches)
        def _():
            attend(
                i, first, last, q_ref, own_ref, all_ref, bias_ref, values, attn, after
            )

    def turn(i, carry):
        some(i, 0, groups // 2)

        @pl.when(i == 0)
        def _():
            for c in range(pieces // 2, pieces):
                pass_on(0, c)
            for c in range(pieces // 2):
                pass_over(0, c)

        @pl.when(i > 0)
        def _():
            b = i - 1

            @pl.when(i == 1)
            def _():
                own_rows(0).wait()

            for g in range(groups):
                attn_copy(b, g).wait_recv()
            for c in range(halves):
                @pl.when(i == 1)
                def _(c=c):
                    for p in range(c * per_half, (c + 1) * per_half):
                        need(0, p)

                send_chunk(0, b, c)

        some(i, groups // 2, groups)

        @pl.when(i == 0)
        def _():
            for c in range(pieces // 2, pieces):
                pass_over(0, c)

        @pl.when(i == 0)
        def _():
            to_mate(1, 0).start()

        @pl.when(i == 2)
        def _():
            to_mate(1, 1).start()
            pages_to_side()

        @pl.when(i == branches - 1)
        def _():
            for c in range(2, pieces):
                to_mate(1, c).start()
            if spots > 2:
                for c in range(pieces):
                    to_mate(2, c).start()
            for c in range(per_half):
                pass_on(1, c)

        @pl.when(i == branches)
        def _():
            pages_to_home()
            for c in range(per_half):
                pass_over(1, c)
            for c in range(per_half, pieces):
                pass_on(1, c)

        return carry

    lax.fori_loop(0, branches + 1, turn, 0)

    def ahead(act, step, c, by):
        later = c + by
        where = step + later // halves
        first = later % halves * per_half

        @pl.when(where < spots)
        def _():
            for p in range(first, first + per_half):
                act(where, p)

    def phase(step, carry):
        own_rows(step).wait()

        @pl.when(step + 2 < spots)
        def _():
            for p in range(pieces):
                to_mate(step + 2, p).start()

        for c in range(halves):
            for p in range(c * per_half, (c + 1) * per_half):
                need(step, p)

            def over(b, inner, c=c):
                @pl.when(step < spots - 1)
                def _():
                    send_chunk(step, b, c)

                @pl.when(step == spots - 1)
                def _():
                    last_chunk(b, c)

                return inner

            lax.fori_loop(0, branches // 2, over, 0)
            ahead(pass_over, step, c, 1)
            ahead(pass_on, step, c, 2)
            lax.fori_loop(branches // 2, branches, over, 0)
        return carry

    lax.fori_loop(1, spots, phase, 0)

    def drain_attn(b, carry):
        for g in range(groups):
            attn_copy(b, g).wait_send()
        return carry

    lax.fori_loop(0, branches, drain_attn, 0)

    def drain_weight(step, carry):
        for c in range(pieces):
            to_mate(step, c).wait_send()
            for k in range(1, chips):
                to_chip(step, c, k).wait_send()
            for k in range(chips):
                to_core(step, c, k).wait_send()
        return carry

    lax.fori_loop(0, spots, drain_weight, 0)

    def drain_chunks(step, carry):
        def over(b, inner):
            for c in range(halves):
                chunk_copy(step, b, c).wait_send()
            return inner

        return lax.fori_loop(0, branches, over, carry)

    lax.fori_loop(0, spots - 1, drain_chunks, 0)
    for k in range(1, chips):
        across(k).wait_send()
    for k in range(chips):
        beside(k).wait_send()
    for k in range(1, spots):
        to_row(k).wait_send()
    to_side.wait_send()
    for part in range(ratio):
        home_local(part).wait()
        for k in range(1, n_pre):
            to_home(k, part).wait_send()
            to_home(k, part).wait_recv()


def settle_kernel(*refs):
    count = (len(refs) - 1) // 2
    sem = refs[-1]
    copies = [
        pltpu.make_async_copy(refs[i], refs[count + i], sem.at[i]) for i in range(count)
    ]
    for copy in copies:
        copy.start()
    for copy in copies:
        copy.wait()


def settle(*arrays):
    anywhere = pl.BlockSpec(memory_space=pl.ANY)
    return pl.pallas_call(
        settle_kernel,
        out_shape=tuple(jax.ShapeDtypeStruct(a.shape, a.dtype) for a in arrays),
        in_specs=[anywhere] * len(arrays),
        out_specs=(anywhere,) * len(arrays),
        scratch_shapes=[pltpu.SemaphoreType.DMA((len(arrays),))],
        name="settle",
    )(*arrays)


def layer(lists, reach, owner, kv, pool, queries, own, weight, n_pre, n_dec):
    branches, page_len, depth = queries.shape
    count = pool.shape[0]
    cols = weight.shape[1] // n_dec
    ratio = n_dec // n_pre
    chips = n_pre // 2
    spots = n_dec // 2
    groups = depth // (PAIR * HD)
    bf16 = jnp.bfloat16
    anywhere = pl.BlockSpec(memory_space=pl.ANY)
    dma = pltpu.SemaphoreType.DMA
    return pl.pallas_call(
        functools.partial(layer_kernel, n_pre, n_dec),
        out_shape=(
            pltpu.VMEM((branches, page_len, cols), bf16),
            pltpu.VMEM((n_pre, page_len, ratio * kv.shape[2]), bf16),
        ),
        in_specs=[SMEM] * 3 + [VMEM] + [anywhere] * 4,
        out_specs=(VMEM, VMEM),
        scratch_shapes=[
            pltpu.VMEM((count * n_pre,) + pool.shape[1:], bf16),
            pltpu.VMEM(queries.shape, bf16),
            pltpu.VMEM(own.shape, bf16),
            pltpu.VMEM((count * n_pre * page_len, 2 * HD), bf16),
            pltpu.VMEM((branches, page_len, 2 * depth), bf16),
            pltpu.VMEM((spots, 2 * depth, cols), bf16),
            pltpu.VMEM((spots, branches, page_len, cols), bf16),
            pltpu.VMEM((spots + 1, branches, page_len, cols), bf16),
            pltpu.VMEM((branches, 1, count * n_pre * page_len), jnp.float32),
            pltpu.VMEM((spots, 2) + kv.shape[1:], bf16),
            pltpu.VMEM((spots, 2) + kv.shape[1:], bf16),
            pltpu.VMEM((2, spots) + kv.shape[1:], bf16),
            dma((3,)),
            dma((spots,)),
            dma((n_pre,)),
            dma((n_pre,)),
            dma((spots,)),
            dma((spots,)),
            dma((1,)),
            dma((2,)),
            dma((n_pre, ratio)),
            dma((n_pre, ratio)),
            dma((branches, groups)),
            dma((branches, groups)),
            dma((spots, WPIECES)),
            dma((spots, WPIECES)),
            dma((spots, WPIECES, chips)),
            dma((spots, WPIECES, chips)),
            dma((spots, WPIECES, chips)),
            dma((spots, WPIECES, chips)),
            dma((spots, branches, CHUNKS)),
            dma((spots + 1, branches, CHUNKS)),
        ],
        compiler_params=pltpu.CompilerParams(
            has_side_effects=True, collective_id=0, vmem_limit_bytes=62 * 2**20
        ),
        name="layer",
    )(lists, reach, owner, kv, pool, queries, own, weight)


def on_device(
    queries, branch_kv, pool_kv, page_lists, anc_len, dec_owner, output_projection_weight
):
    n_pre = lax.axis_size("pre")
    n_dec = lax.axis_size("dec")
    dec_idx = lax.axis_index("dec")
    kv_cols = pool_kv.shape[2]
    if kv_cols < 2 * HD:
        other_pool, other_own = from_partner((pool_kv, branch_kv), "dec", 0)
        first_half = dec_idx % 2 == 0
        pool = jnp.where(
            first_half,
            jnp.concatenate([pool_kv, other_pool], 2),
            jnp.concatenate([other_pool, pool_kv], 2),
        )
        own = jnp.where(
            first_half,
            jnp.concatenate([branch_kv, other_own], 2),
            jnp.concatenate([other_own, branch_kv], 2),
        )
    else:
        pool, own = pool_kv, branch_kv

    layer_out, decode_pages = layer(
        page_lists,
        anc_len,
        dec_owner,
        branch_kv,
        pool,
        queries,
        own,
        output_projection_weight,
        n_pre,
        n_dec,
    )
    return (layer_out, decode_pages)


def solution(mesh):
    in_specs = (
        P("pre", None, "dec"),
        P("pre", None, "dec"),
        P("pre", None, "dec"),
        P(),
        P(),
        P(),
        P("dec", None),
    )
    out_specs = (P("pre", None, "dec"), P("dec", None, "pre"))
    return jax.shard_map(
        on_device, mesh=mesh, in_specs=in_specs, out_specs=out_specs, check_vma=False
    )
```

```python
import functools
import math

import jax
import jax.numpy as jnp
from jax import lax
from jax.experimental import pallas as pl
from jax.experimental.pallas import tpu as pltpu
from jax.sharding import PartitionSpec as P

HD = 128
MASKED = -1e30
SCALE = HD**-0.5 * math.log2(math.e)
MESH = pl.DeviceIdType.MESH
VMEM = pl.BlockSpec(memory_space=pltpu.VMEM)
SMEM = pl.BlockSpec(memory_space=pltpu.SMEM)
PAIR = 2
WPIECES = 4
CHUNKS = 2


def from_partner(value, axis, stride):
    mask = 2**stride
    pairs = [(source, source ^ mask) for source in range(lax.axis_size(axis))]
    return lax.ppermute(value, axis, pairs)


def load_values(pool_ref, values):
    pages, page_len, _ = pool_ref.shape
    values[:, :HD] = pool_ref[:, :, HD:].reshape(pages * page_len, HD)
    values[:, HD:] = jnp.ones((pages * page_len, HD), values.dtype)


def attend(branch, g, q_ref, own_ref, pool_ref, bias_ref, values, attn):
    pages, page_len, _ = pool_ref.shape
    keys = pool_ref[:, :, :HD].reshape(pages * page_len, HD)
    own_keys = own_ref[branch, :, :HD]
    own_values = own_ref[branch, :, HD:]
    own_values = jnp.concatenate([own_values, jnp.ones_like(own_values)], 1)
    row = lax.broadcasted_iota(jnp.int32, (page_len, page_len), 0)
    col = lax.broadcasted_iota(jnp.int32, (page_len, page_len), 1)
    causal = jnp.where(col <= row, 0.0, MASKED)
    causal = jnp.concatenate([causal] * PAIR, 0)
    bias = bias_ref[branch]
    nt = (((1,), (1,)), ((), ()))
    start = pl.multiple_of(g * PAIR * HD, PAIR * HD)
    q = q_ref[branch, :, pl.ds(start, PAIR * HD)]
    q = jnp.concatenate([q[:, i * HD : (i + 1) * HD] for i in range(PAIR)], 0)
    far = lax.dot_general(q, keys, nt, preferred_element_type=jnp.float32) + bias
    near = lax.dot_general(q, own_keys, nt, preferred_element_type=jnp.float32) + causal
    top = jnp.maximum(
        jnp.max(far, axis=-1, keepdims=True), jnp.max(near, axis=-1, keepdims=True)
    )
    top = top * SCALE
    far = jnp.exp2(far * SCALE - top).astype(jnp.bfloat16)
    near = jnp.exp2(near * SCALE - top).astype(jnp.bfloat16)
    out = jnp.dot(far, values[...], preferred_element_type=jnp.float32)
    out = out + jnp.dot(near, own_values, preferred_element_type=jnp.float32)
    out = (out[:, :HD] / out[:, HD:]).astype(jnp.bfloat16)
    for i in range(PAIR):
        attn[branch, :, pl.ds(start + i * HD, HD)] = out[i * page_len : (i + 1) * page_len]


def layer_kernel(
    n_pre,
    n_dec,
    lists_ref,
    reach_ref,
    owner_ref,
    kv_ref,
    pool_ref,
    q_hbm,
    own_hbm,
    w_ref,
    out_ref,
    pages_ref,
    all_ref,
    q_ref,
    own_ref,
    values,
    attn,
    wv,
    sent,
    got,
    bias_ref,
    bucket_ref,
    row_ref,
    block_ref,
    load_sem,
    wsem,
    psend,
    precv,
    bsend,
    brecv,
    msend,
    mrecv,
    hsend,
    hrecv,
    asend,
    arecv,
    ysend,
    yrecv,
    xsend,
    xrecv,
    csend,
    crecv,
    ssem,
    rsem,
):
    pre = lax.axis_index("pre")
    dec = lax.axis_index("dec")
    branches, page_len, cols = out_ref.shape
    depth = w_ref.shape[0]
    count = pool_ref.shape[0]
    width = kv_ref.shape[2]
    ratio = n_dec // n_pre
    chips = n_pre // 2
    chip = pre // 2
    core = lax.rem(pre, 2)
    spots = n_dec // 2
    spot = dec // 2
    side = lax.rem(dec, 2)
    mate = dec + 1 - 2 * side
    share = depth // n_pre
    pieces = WPIECES
    piece = cols // pieces
    halves = CHUNKS
    half = cols // halves
    per_half = pieces // halves
    groups = depth // (PAIR * HD)
    low = 2 * spot < spots

    def target(step):
        outer = spots - 1 - spot
        rising = jnp.where(step < outer, spots - 1 - step, step - outer)
        falling = jnp.where(step < spot, step, spots - 1 - step + spot)
        return jnp.where(low, rising, falling)

    def block_of(device):
        return pl.ds(device * count, count)

    def across(k):
        return pltpu.make_async_remote_copy(
            src_ref=pool_ref,
            dst_ref=all_ref.at[block_of(pre)],
            send_sem=psend.at[k],
            recv_sem=precv.at[k],
            device_id={"pre": lax.rem(chip + k, chips) * 2 + core},
            device_id_type=MESH,
        )

    def beside(k):
        where = all_ref.at[block_of(lax.rem(chip + chips - k, chips) * 2 + core)]
        return pltpu.make_async_remote_copy(
            src_ref=pool_ref if k == 0 else where,
            dst_ref=where,
            send_sem=psend.at[chips + k],
            recv_sem=precv.at[chips + k],
            device_id={"pre": chip * 2 + 1 - core},
            device_id_type=MESH,
        )

    def own_rows(step):
        t = target(step)
        start = pl.multiple_of((2 * t + side) * cols, cols)
        return pltpu.make_async_copy(
            w_ref.at[:, pl.ds(start, cols)], wv.at[t, pl.ds(0, depth)], wsem.at[step]
        )

    def share_of(device, step, c):
        rows = pl.ds(pl.multiple_of(depth + device * share, 16), share)
        return wv.at[target(step), rows, pl.ds(pl.multiple_of(c * piece, piece), piece)]

    def to_mate(step, c):
        start = pl.multiple_of((2 * target(step) + 1 - side) * cols + c * piece, piece)
        rows = pl.ds(pl.multiple_of(pre * share, 16), share)
        return pltpu.make_async_remote_copy(
            src_ref=w_ref.at[rows, pl.ds(start, piece)],
            dst_ref=share_of(pre, step, c),
            send_sem=ysend.at[step, c],
            recv_sem=yrecv.at[step, c],
            device_id={"dec": mate},
            device_id_type=MESH,
        )

    def to_chip(step, c, k):
        return pltpu.make_async_remote_copy(
            src_ref=share_of(pre, step, c),
            dst_ref=share_of(pre, step, c),
            send_sem=xsend.at[step, c, k],
            recv_sem=xrecv.at[step, c, k],
            device_id={"pre": lax.rem(chip + k, chips) * 2 + core},
            device_id_type=MESH,
        )

    def to_core(step, c, k):
        where = share_of(lax.rem(chip + chips - k, chips) * 2 + core, step, c)
        return pltpu.make_async_remote_copy(
            src_ref=where,
            dst_ref=where,
            send_sem=csend.at[step, c, k],
            recv_sem=crecv.at[step, c, k],
            device_id={"pre": chip * 2 + 1 - core},
            device_id_type=MESH,
        )

    def pass_on(step, c):
        to_mate(step, c).wait_recv()
        for k in range(1, chips):
            to_chip(step, c, k).start()
        to_core(step, c, 0).start()

    def pass_over(step, c):
        for k in range(1, chips):
            to_chip(step, c, k).wait_recv()
            to_core(step, c, k).start()

    def need(step, c):
        for k in range(chips):
            to_core(step, c, k).wait_recv()

    def attn_copy(b, g):
        start = pl.multiple_of(g * PAIR * HD, PAIR * HD)
        return pltpu.make_async_remote_copy(
            src_ref=attn.at[b, :, pl.ds(start, PAIR * HD)],
            dst_ref=attn.at[b, :, pl.ds(depth + start, PAIR * HD)],
            send_sem=asend.at[b, g],
            recv_sem=arecv.at[b, g],
            device_id={"dec": mate},
            device_id_type=MESH,
        )

    def at_half(c):
        return pl.ds(pl.multiple_of(c * half, half), half)

    def arrival(slot, b, c):
        where = got.at[slot, b, :, at_half(c)]
        return pltpu.make_async_copy(where, where, rsem.at[slot, b, c])

    def chunk_copy(step, b, c):
        t = target(step)
        onward = t > spot
        slot = jnp.where(t == spot - 1, spots, t)
        return pltpu.make_async_remote_copy(
            src_ref=sent.at[t, b, :, at_half(c)],
            dst_ref=got.at[slot, b, :, at_half(c)],
            send_sem=ssem.at[step, b, c],
            recv_sem=rsem.at[slot, b, c],
            device_id={"dec": jnp.where(onward, dec + 2, dec - 2)},
            device_id_type=MESH,
        )

    def send_chunk(step, b, c):
        t = target(step)
        relayed = jnp.where(t > spot, spot > 0, spot < spots - 1)

        @pl.when(relayed)
        def _():
            arrival(t, b, c).wait()

        total = jnp.dot(attn[b], wv[t, :, at_half(c)], preferred_element_type=jnp.float32)
        total = total + got[t, b, :, at_half(c)].astype(jnp.float32)
        sent[t, b, :, at_half(c)] = total.astype(jnp.bfloat16)
        chunk_copy(step, b, c).start()

    def last_chunk(b, c):
        @pl.when(spot > 0)
        def _():
            arrival(spot, b, c).wait()

        @pl.when(spot < spots - 1)
        def _():
            arrival(spots, b, c).wait()

        total = jnp.dot(attn[b], wv[spot, :, at_half(c)], preferred_element_type=jnp.float32)
        total = total + got[spot, b, :, at_half(c)].astype(jnp.float32)
        total = total + got[spots, b, :, at_half(c)].astype(jnp.float32)
        out_ref[b, :, at_half(c)] = total.astype(jnp.bfloat16)

    def to_row(k):
        where = lax.rem(spot + k, spots)
        return pltpu.make_async_remote_copy(
            src_ref=bucket_ref.at[where],
            dst_ref=row_ref.at[spot],
            send_sem=bsend.at[k],
            recv_sem=brecv.at[k],
            device_id={"dec": 2 * where + side},
            device_id_type=MESH,
        )

    row_local = pltpu.make_async_copy(bucket_ref.at[spot], row_ref.at[spot], brecv.at[0])
    to_side = pltpu.make_async_remote_copy(
        src_ref=row_ref.at[:, 1 - side],
        dst_ref=block_ref.at[side],
        send_sem=msend.at[0],
        recv_sem=mrecv.at[0],
        device_id={"dec": mate},
        device_id_type=MESH,
    )
    side_local = pltpu.make_async_copy(row_ref.at[:, side], block_ref.at[side], mrecv.at[1])

    def home_parts(k, part):
        home = lax.rem(pre + k, n_pre)
        source = home * ratio + part
        src = block_ref.at[lax.rem(source, 2), source // 2]
        return home, src, pages_ref.at[pre, :, pl.ds(part * width, width)]

    def to_home(k, part):
        home, src, dst = home_parts(k, part)
        return pltpu.make_async_remote_copy(
            src_ref=src,
            dst_ref=dst,
            send_sem=hsend.at[k, part],
            recv_sem=hrecv.at[k, part],
            device_id={"pre": home},
            device_id_type=MESH,
        )

    def home_local(part):
        _, src, dst = home_parts(0, part)
        return pltpu.make_async_copy(src, dst, hrecv.at[0, part])

    def pages_to_side():
        for k in range(1, spots):
            to_row(k).wait_recv()
        row_local.wait()
        to_side.start()
        side_local.start()

    def pages_to_home():
        to_side.wait_recv()
        side_local.wait()
        for part in range(ratio):
            home_local(part).start()
            for k in range(1, n_pre):
                to_home(k, part).start()

    barrier = pltpu.get_barrier_semaphore()
    for k in range(1, n_pre):
        pl.semaphore_signal(
            barrier, 1, device_id={"pre": lax.rem(pre + k, n_pre)}, device_id_type=MESH
        )
    pl.semaphore_signal(barrier, 1, device_id={"dec": mate}, device_id_type=MESH)
    for k in range(1, spots):
        pl.semaphore_signal(
            barrier,
            1,
            device_id={"dec": 2 * lax.rem(spot + k, spots) + side},
            device_id_type=MESH,
        )
    loads = [
        pltpu.make_async_copy(pool_ref, all_ref.at[block_of(pre)], load_sem.at[0]),
        pltpu.make_async_copy(q_hbm, q_ref, load_sem.at[1]),
        pltpu.make_async_copy(own_hbm, own_ref, load_sem.at[2]),
    ]
    for copy in loads:
        copy.start()
    own_rows(0).start()
    pl.semaphore_wait(barrier, n_pre + spots - 1)

    for k in range(1, chips):
        across(k).start()
    beside(0).start()
    for c in range(pieces):
        to_mate(0, c).start()
    first = pre * branches
    for o in range(n_dec):
        bucket = jnp.zeros(kv_ref.shape[1:], kv_ref.dtype)
        for b in range(branches):
            bucket = jnp.where(owner_ref[first + b] == o, kv_ref[b], bucket)
        bucket_ref[o // 2, o % 2] = bucket
    for k in range(1, spots):
        to_row(k).start()
    row_local.start()

    def mask(b, carry):
        visible = jnp.zeros((count * n_pre, page_len), jnp.int32)
        page = lax.broadcasted_iota(jnp.int32, visible.shape, 0)
        token = lax.broadcasted_iota(jnp.int32, visible.shape, 1)
        for slot in range(lists_ref.shape[1]):
            shown = reach_ref[first + b] - slot * page_len
            visible = jnp.where(page == lists_ref[first + b, slot], shown, visible)
        bias = jnp.where(token < visible, 0.0, MASKED).astype(jnp.float32)
        for p in range(count * n_pre):
            bias_ref[b, :, p * page_len : (p + 1) * page_len] = bias[p : p + 1]
        return carry

    lax.fori_loop(0, branches, mask, 0)

    @pl.when(spot == 0)
    def _():
        def clear(t, carry):
            got[t] = jnp.zeros(got.shape[1:], got.dtype)
            return carry

        lax.fori_loop(0, spots, clear, 0)

    @pl.when(spot == spots - 1)
    def _():
        def clear(t, carry):
            got[t + t // (spots - 1)] = jnp.zeros(got.shape[1:], got.dtype)
            return carry

        lax.fori_loop(0, spots, clear, 0)

    pass_on(0, 0)
    for k in range(1, chips):
        across(k).wait_recv()
        beside(k).start()

    pass_on(0, 1)
    for copy in loads:
        copy.wait()
    for k in range(chips):
        beside(k).wait_recv()
    load_values(all_ref, values)

    def load_rest(step, carry):
        own_rows(step).start()
        return carry

    lax.fori_loop(1, spots, load_rest, 0)

    def first_chunks(b):
        for g in range(groups):
            attn_copy(b, g).wait_recv()
        for c in range(halves):
            @pl.when(b == 0)
            def _(c=c):
                for p in range(c * per_half, (c + 1) * per_half):
                    need(0, p)

            send_chunk(0, b, c)

    total_groups = branches * groups

    def at(n, where):
        def run(act):
            @pl.when(n == where)
            def _():
                act()

        return run

    def turn(n, carry):
        b = n // groups
        g = lax.rem(n, groups)
        attend(b, g, q_ref, own_ref, all_ref, bias_ref, values, attn)
        attn_copy(b, g).start()

        @at(n, 0)
        def _():
            pass_on(0, 2)
            pass_over(0, 0)

        @at(n, 2)
        def _():
            pass_on(0, 3)
            pass_over(0, 1)

        @at(n, 4)
        def _():
            pass_over(0, 2)
            to_mate(1, 0).start()

        @at(n, 5)
        def _():
            own_rows(0).wait()
            pass_over(0, 3)

        @pl.when(jnp.logical_and(n >= groups, g == groups // 2 - 1))
        def _():
            first_chunks(b - 1)

        @at(n, 11)
        def _():
            to_mate(1, 1).start()
            pass_on(1, 0)

        @at(n, total_groups - 1)
        def _():
            for c in range(2, pieces):
                to_mate(1, c).start()
            if spots > 2:
                for c in range(pieces):
                    to_mate(2, c).start()
            pass_on(1, 1)
            pass_over(1, 0)

        return carry

    lax.fori_loop(0, total_groups, turn, 0)
    first_chunks(branches - 1)
    pass_over(1, 1)
    for c in range(per_half, pieces):
        pass_on(1, c)

    def ahead(act, step, c, by):
        later = c + by
        where = step + later // halves
        first = later % halves * per_half

        @pl.when(where < spots)
        def _():
            for p in range(first, first + per_half):
                act(where, p)

    def phase(step, carry):
        own_rows(step).wait()

        @pl.when(step + 2 < spots)
        def _():
            for p in range(pieces):
                to_mate(step + 2, p).start()

        @pl.when(step == spots - 2)
        def _():
            pages_to_side()

        @pl.when(step == spots - 1)
        def _():
            pages_to_home()

        for c in range(halves):
            for p in range(c * per_half, (c + 1) * per_half):
                need(step, p)

            def over(b, inner, c=c):
                @pl.when(step < spots - 1)
                def _():
                    send_chunk(step, b, c)

                @pl.when(step == spots - 1)
                def _():
                    last_chunk(b, c)

                return inner

            lax.fori_loop(0, branches // 2, over, 0)
            ahead(pass_over, step, c, 1)
            ahead(pass_on, step, c, 2)
            lax.fori_loop(branches // 2, branches, over, 0)
        return carry

    lax.fori_loop(1, spots, phase, 0)

    def drain_attn(b, carry):
        for g in range(groups):
            attn_copy(b, g).wait_send()
        return carry

    lax.fori_loop(0, branches, drain_attn, 0)

    def drain_weight(step, carry):
        for c in range(pieces):
            to_mate(step, c).wait_send()
            for k in range(1, chips):
                to_chip(step, c, k).wait_send()
            for k in range(chips):
                to_core(step, c, k).wait_send()
        return carry

    lax.fori_loop(0, spots, drain_weight, 0)

    def drain_chunks(step, carry):
        def over(b, inner):
            for c in range(halves):
                chunk_copy(step, b, c).wait_send()
            return inner

        return lax.fori_loop(0, branches, over, carry)

    lax.fori_loop(0, spots - 1, drain_chunks, 0)
    for k in range(1, chips):
        across(k).wait_send()
    for k in range(chips):
        beside(k).wait_send()
    for k in range(1, spots):
        to_row(k).wait_send()
    to_side.wait_send()
    for part in range(ratio):
        home_local(part).wait()
        for k in range(1, n_pre):
            to_home(k, part).wait_send()
            to_home(k, part).wait_recv()


def settle_kernel(*refs):
    count = (len(refs) - 1) // 2
    sem = refs[-1]
    copies = [
        pltpu.make_async_copy(refs[i], refs[count + i], sem.at[i]) for i in range(count)
    ]
    for copy in copies:
        copy.start()
    for copy in copies:
        copy.wait()


def settle(*arrays):
    anywhere = pl.BlockSpec(memory_space=pl.ANY)
    return pl.pallas_call(
        settle_kernel,
        out_shape=tuple(jax.ShapeDtypeStruct(a.shape, a.dtype) for a in arrays),
        in_specs=[anywhere] * len(arrays),
        out_specs=(anywhere,) * len(arrays),
        scratch_shapes=[pltpu.SemaphoreType.DMA((len(arrays),))],
        name="settle",
    )(*arrays)


def layer(lists, reach, owner, kv, pool, queries, own, weight, n_pre, n_dec):
    branches, page_len, depth = queries.shape
    count = pool.shape[0]
    cols = weight.shape[1] // n_dec
    ratio = n_dec // n_pre
    chips = n_pre // 2
    spots = n_dec // 2
    groups = depth // (PAIR * HD)
    bf16 = jnp.bfloat16
    anywhere = pl.BlockSpec(memory_space=pl.ANY)
    dma = pltpu.SemaphoreType.DMA
    return pl.pallas_call(
        functools.partial(layer_kernel, n_pre, n_dec),
        out_shape=(
            pltpu.VMEM((branches, page_len, cols), bf16),
            pltpu.VMEM((n_pre, page_len, ratio * kv.shape[2]), bf16),
        ),
        in_specs=[SMEM] * 3 + [VMEM] + [anywhere] * 4,
        out_specs=(VMEM, VMEM),
        scratch_shapes=[
            pltpu.VMEM((count * n_pre,) + pool.shape[1:], bf16),
            pltpu.VMEM(queries.shape, bf16),
            pltpu.VMEM(own.shape, bf16),
            pltpu.VMEM((count * n_pre * page_len, 2 * HD), bf16),
            pltpu.VMEM((branches, page_len, 2 * depth), bf16),
            pltpu.VMEM((spots, 2 * depth, cols), bf16),
            pltpu.VMEM((spots, branches, page_len, cols), bf16),
            pltpu.VMEM((spots + 1, branches, page_len, cols), bf16),
            pltpu.VMEM((branches, 1, count * n_pre * page_len), jnp.float32),
            pltpu.VMEM((spots, 2) + kv.shape[1:], bf16),
            pltpu.VMEM((spots, 2) + kv.shape[1:], bf16),
            pltpu.VMEM((2, spots) + kv.shape[1:], bf16),
            dma((3,)),
            dma((spots,)),
            dma((n_pre,)),
            dma((n_pre,)),
            dma((spots,)),
            dma((spots,)),
            dma((1,)),
            dma((2,)),
            dma((n_pre, ratio)),
            dma((n_pre, ratio)),
            dma((branches, groups)),
            dma((branches, groups)),
            dma((spots, WPIECES)),
            dma((spots, WPIECES)),
            dma((spots, WPIECES, chips)),
            dma((spots, WPIECES, chips)),
            dma((spots, WPIECES, chips)),
            dma((spots, WPIECES, chips)),
            dma((spots, branches, CHUNKS)),
            dma((spots + 1, branches, CHUNKS)),
        ],
        compiler_params=pltpu.CompilerParams(
            has_side_effects=True, collective_id=0, vmem_limit_bytes=62 * 2**20
        ),
        name="layer",
    )(lists, reach, owner, kv, pool, queries, own, weight)


def on_device(
    queries, branch_kv, pool_kv, page_lists, anc_len, dec_owner, output_projection_weight
):
    n_pre = lax.axis_size("pre")
    n_dec = lax.axis_size("dec")
    dec_idx = lax.axis_index("dec")
    kv_cols = pool_kv.shape[2]
    if kv_cols < 2 * HD:
        other_pool, other_own = from_partner((pool_kv, branch_kv), "dec", 0)
        first_half = dec_idx % 2 == 0
        pool = jnp.where(
            first_half,
            jnp.concatenate([pool_kv, other_pool], 2),
            jnp.concatenate([other_pool, pool_kv], 2),
        )
        own = jnp.where(
            first_half,
            jnp.concatenate([branch_kv, other_own], 2),
            jnp.concatenate([other_own, branch_kv], 2),
        )
    else:
        pool, own = pool_kv, branch_kv

    layer_out, decode_pages = layer(
        page_lists,
        anc_len,
        dec_owner,
        branch_kv,
        pool,
        queries,
        own,
        output_projection_weight,
        n_pre,
        n_dec,
    )
    return (layer_out, decode_pages)


def solution(mesh):
    in_specs = (
        P("pre", None, "dec"),
        P("pre", None, "dec"),
        P("pre", None, "dec"),
        P(),
        P(),
        P(),
        P("dec", None),
    )
    out_specs = (P("pre", None, "dec"), P("dec", None, "pre"))
    return jax.shard_map(
        on_device, mesh=mesh, in_specs=in_specs, out_specs=out_specs, check_vma=False
    )
```

```python
import functools
import math

import jax
import jax.numpy as jnp
from jax import lax
from jax.experimental import pallas as pl
from jax.experimental.pallas import tpu as pltpu
from jax.sharding import PartitionSpec as P

HD = 128
MASKED = -1e30
SCALE = HD**-0.5 * math.log2(math.e)
MESH = pl.DeviceIdType.MESH
VMEM = pl.BlockSpec(memory_space=pltpu.VMEM)
SMEM = pl.BlockSpec(memory_space=pltpu.SMEM)
PAIR = 2
BLOCK = 2
PIECES = 4


def from_partner(value, axis, stride):
    mask = 2**stride
    pairs = [(source, source ^ mask) for source in range(lax.axis_size(axis))]
    return lax.ppermute(value, axis, pairs)


def load_values(pool_ref, values):
    pages, page_len, _ = pool_ref.shape
    values[:, :HD] = pool_ref[:, :, HD:].reshape(pages * page_len, HD)
    values[:, HD:] = jnp.ones((pages * page_len, HD), values.dtype)


def attend(branch, start, block, q_ref, own_ref, pool_ref, bias_ref, values, attn):
    pages, page_len, _ = pool_ref.shape
    keys = pool_ref[:, :, :HD].reshape(pages * page_len, HD)
    own_keys = own_ref[branch, :, :HD]
    own_values = own_ref[branch, :, HD:]
    own_values = jnp.concatenate([own_values, jnp.ones_like(own_values)], 1)
    row = lax.broadcasted_iota(jnp.int32, (page_len, page_len), 0)
    col = lax.broadcasted_iota(jnp.int32, (page_len, page_len), 1)
    causal = jnp.where(col <= row, 0.0, MASKED)
    causal = jnp.concatenate([causal] * PAIR, 0)
    bias = bias_ref[branch]
    nt = (((1,), (1,)), ((), ()))
    outs = []
    for g in range(block):
        q = q_ref[branch, :, pl.ds(start + g * PAIR * HD, PAIR * HD)]
        q = jnp.concatenate([q[:, i * HD : (i + 1) * HD] for i in range(PAIR)], 0)
        far = lax.dot_general(q, keys, nt, preferred_element_type=jnp.float32) + bias
        near = lax.dot_general(q, own_keys, nt, preferred_element_type=jnp.float32) + causal
        top = jnp.maximum(
            jnp.max(far, axis=-1, keepdims=True), jnp.max(near, axis=-1, keepdims=True)
        )
        top = top * SCALE
        far = jnp.exp2(far * SCALE - top).astype(jnp.bfloat16)
        near = jnp.exp2(near * SCALE - top).astype(jnp.bfloat16)
        out = jnp.dot(far, values[...], preferred_element_type=jnp.float32)
        out = out + jnp.dot(near, own_values, preferred_element_type=jnp.float32)
        out = (out[:, :HD] / out[:, HD:]).astype(jnp.bfloat16)
        outs.extend(out[i * page_len : (i + 1) * page_len] for i in range(PAIR))
    for i, out in enumerate(outs):
        attn[branch, :, pl.ds(start + i * HD, HD)] = out


def layer_kernel(
    n_pre,
    n_dec,
    lists_ref,
    reach_ref,
    owner_ref,
    kv_ref,
    pool_ref,
    q_hbm,
    own_hbm,
    w_ref,
    out_ref,
    pages_ref,
    all_ref,
    q_ref,
    own_ref,
    values,
    attn,
    wv,
    sent,
    got,
    bias_ref,
    bucket_ref,
    row_ref,
    block_ref,
    load_sem,
    wsem,
    psend,
    precv,
    bsend,
    brecv,
    msend,
    mrecv,
    hsend,
    hrecv,
    asend,
    arecv,
    ysend,
    yrecv,
    xsend,
    xrecv,
    csend,
    crecv,
    ssem,
    rsem,
):
    pre = lax.axis_index("pre")
    dec = lax.axis_index("dec")
    branches, page_len, cols = out_ref.shape
    depth = w_ref.shape[0]
    count = pool_ref.shape[0]
    width = kv_ref.shape[2]
    ratio = n_dec // n_pre
    chips = n_pre // 2
    chip = pre // 2
    core = lax.rem(pre, 2)
    spots = n_dec // 2
    spot = dec // 2
    side = lax.rem(dec, 2)
    mate = dec + 1 - 2 * side
    share = depth // n_pre
    pieces = PIECES
    piece = cols // pieces
    block = min(BLOCK, depth // (PAIR * HD))
    span = block * PAIR * HD
    blocks = depth // span
    low = 2 * spot < spots

    def target(step):
        near = jnp.where(low, spot, spots - 1 - spot)
        paired = jnp.where(step % 2 == 0, spots - 1 - step // 2, step // 2)
        t = jnp.where(step < 2 * near, paired, spots - 1 - step + near)
        return jnp.where(low, t, spots - 1 - t)

    def block_of(device):
        return pl.ds(device * count, count)

    def across(k):
        return pltpu.make_async_remote_copy(
            src_ref=pool_ref,
            dst_ref=all_ref.at[block_of(pre)],
            send_sem=psend.at[k],
            recv_sem=precv.at[k],
            device_id={"pre": lax.rem(chip + k, chips) * 2 + core},
            device_id_type=MESH,
        )

    def beside(k):
        where = all_ref.at[block_of(lax.rem(chip + chips - k, chips) * 2 + core)]
        return pltpu.make_async_remote_copy(
            src_ref=pool_ref if k == 0 else where,
            dst_ref=where,
            send_sem=psend.at[chips + k],
            recv_sem=precv.at[chips + k],
            device_id={"pre": chip * 2 + 1 - core},
            device_id_type=MESH,
        )

    def own_rows(step):
        t = target(step)
        start = pl.multiple_of((2 * t + side) * cols, cols)
        return pltpu.make_async_copy(
            w_ref.at[:, pl.ds(start, cols)], wv.at[t, pl.ds(0, depth)], wsem.at[step]
        )

    def share_of(device, step, c):
        rows = pl.ds(pl.multiple_of(depth + device * share, 16), share)
        return wv.at[target(step), rows, pl.ds(pl.multiple_of(c * piece, piece), piece)]

    def to_mate(step, c):
        start = pl.multiple_of((2 * target(step) + 1 - side) * cols + c * piece, piece)
        rows = pl.ds(pl.multiple_of(pre * share, 16), share)
        return pltpu.make_async_remote_copy(
            src_ref=w_ref.at[rows, pl.ds(start, piece)],
            dst_ref=share_of(pre, step, c),
            send_sem=ysend.at[step, c],
            recv_sem=yrecv.at[step, c],
            device_id={"dec": mate},
            device_id_type=MESH,
        )

    def to_chip(step, c, k):
        return pltpu.make_async_remote_copy(
            src_ref=share_of(pre, step, c),
            dst_ref=share_of(pre, step, c),
            send_sem=xsend.at[step, c, k],
            recv_sem=xrecv.at[step, c, k],
            device_id={"pre": lax.rem(chip + k, chips) * 2 + core},
            device_id_type=MESH,
        )

    def to_core(step, c, k):
        where = share_of(lax.rem(chip + chips - k, chips) * 2 + core, step, c)
        return pltpu.make_async_remote_copy(
            src_ref=where,
            dst_ref=where,
            send_sem=csend.at[step, c, k],
            recv_sem=crecv.at[step, c, k],
            device_id={"pre": chip * 2 + 1 - core},
            device_id_type=MESH,
        )

    def pass_on(step, c):
        to_mate(step, c).wait_recv()
        for k in range(1, chips):
            to_chip(step, c, k).start()
        to_core(step, c, 0).start()

    def pass_over(step, c):
        for k in range(1, chips):
            to_chip(step, c, k).wait_recv()
            to_core(step, c, k).start()

    def need(step, c):
        for k in range(chips):
            to_core(step, c, k).wait_recv()

    def attn_copy(b, g):
        start = pl.multiple_of(g * span, span)
        return pltpu.make_async_remote_copy(
            src_ref=attn.at[b, :, pl.ds(start, span)],
            dst_ref=attn.at[b, :, pl.ds(depth + start, span)],
            send_sem=asend.at[b, g],
            recv_sem=arecv.at[b, g],
            device_id={"dec": mate},
            device_id_type=MESH,
        )

    def at_piece(c):
        return pl.ds(pl.multiple_of(c * piece, piece), piece)

    def arrival(slot, b, c):
        where = got.at[slot, b, :, at_piece(c)]
        return pltpu.make_async_copy(where, where, rsem.at[slot, b, c])

    def chunk_copy(step, b, c):
        t = target(step)
        onward = t > spot
        slot = jnp.where(t == spot - 1, spots, t)
        return pltpu.make_async_remote_copy(
            src_ref=sent.at[t, b, :, at_piece(c)],
            dst_ref=got.at[slot, b, :, at_piece(c)],
            send_sem=ssem.at[step, b, c],
            recv_sem=rsem.at[slot, b, c],
            device_id={"dec": jnp.where(onward, dec + 2, dec - 2)},
            device_id_type=MESH,
        )

    def send_chunk(step, b, c):
        t = target(step)
        relayed = jnp.where(t > spot, spot > 0, spot < spots - 1)

        @pl.when(relayed)
        def _():
            arrival(t, b, c).wait()

        total = jnp.dot(attn[b], wv[t, :, at_piece(c)], preferred_element_type=jnp.float32)
        total = total + got[t, b, :, at_piece(c)].astype(jnp.float32)
        sent[t, b, :, at_piece(c)] = total.astype(jnp.bfloat16)
        chunk_copy(step, b, c).start()

    def last_chunk(b, c):
        @pl.when(spot > 0)
        def _():
            arrival(spot, b, c).wait()

        @pl.when(spot < spots - 1)
        def _():
            arrival(spots, b, c).wait()

        total = jnp.dot(attn[b], wv[spot, :, at_piece(c)], preferred_element_type=jnp.float32)
        total = total + got[spot, b, :, at_piece(c)].astype(jnp.float32)
        total = total + got[spots, b, :, at_piece(c)].astype(jnp.float32)
        out_ref[b, :, at_piece(c)] = total.astype(jnp.bfloat16)

    def to_row(k):
        where = lax.rem(spot + k, spots)
        return pltpu.make_async_remote_copy(
            src_ref=bucket_ref.at[where],
            dst_ref=row_ref.at[spot],
            send_sem=bsend.at[k],
            recv_sem=brecv.at[k],
            device_id={"dec": 2 * where + side},
            device_id_type=MESH,
        )

    row_local = pltpu.make_async_copy(bucket_ref.at[spot], row_ref.at[spot], brecv.at[0])
    to_side = pltpu.make_async_remote_copy(
        src_ref=row_ref.at[:, 1 - side],
        dst_ref=block_ref.at[side],
        send_sem=msend.at[0],
        recv_sem=mrecv.at[0],
        device_id={"dec": mate},
        device_id_type=MESH,
    )
    side_local = pltpu.make_async_copy(row_ref.at[:, side], block_ref.at[side], mrecv.at[1])

    def home_parts(k, part):
        home = lax.rem(pre + k, n_pre)
        source = home * ratio + part
        src = block_ref.at[lax.rem(source, 2), source // 2]
        return home, src, pages_ref.at[pre, :, pl.ds(part * width, width)]

    def to_home(k, part):
        home, src, dst = home_parts(k, part)
        return pltpu.make_async_remote_copy(
            src_ref=src,
            dst_ref=dst,
            send_sem=hsend.at[k, part],
            recv_sem=hrecv.at[k, part],
            device_id={"pre": home},
            device_id_type=MESH,
        )

    def home_local(part):
        _, src, dst = home_parts(0, part)
        return pltpu.make_async_copy(src, dst, hrecv.at[0, part])

    def pages_to_side():
        for k in range(1, spots):
            to_row(k).wait_recv()
        row_local.wait()
        to_side.start()
        side_local.start()

    def pages_to_home():
        to_side.wait_recv()
        side_local.wait()
        for part in range(ratio):
            home_local(part).start()
            for k in range(1, n_pre):
                to_home(k, part).start()

    barrier = pltpu.get_barrier_semaphore()
    for k in range(1, n_pre):
        pl.semaphore_signal(
            barrier, 1, device_id={"pre": lax.rem(pre + k, n_pre)}, device_id_type=MESH
        )
    pl.semaphore_signal(barrier, 1, device_id={"dec": mate}, device_id_type=MESH)
    for k in range(1, spots):
        pl.semaphore_signal(
            barrier,
            1,
            device_id={"dec": 2 * lax.rem(spot + k, spots) + side},
            device_id_type=MESH,
        )
    loads = [
        pltpu.make_async_copy(pool_ref, all_ref.at[block_of(pre)], load_sem.at[0]),
        pltpu.make_async_copy(q_hbm, q_ref, load_sem.at[1]),
        pltpu.make_async_copy(own_hbm, own_ref, load_sem.at[2]),
    ]
    for copy in loads:
        copy.start()
    own_rows(0).start()
    pl.semaphore_wait(barrier, n_pre + spots - 1)

    for k in range(1, chips):
        across(k).start()
    beside(0).start()
    for c in range(pieces):
        to_mate(0, c).start()
    first = pre * branches
    for o in range(n_dec):
        bucket = jnp.zeros(kv_ref.shape[1:], kv_ref.dtype)
        for b in range(branches):
            bucket = jnp.where(owner_ref[first + b] == o, kv_ref[b], bucket)
        bucket_ref[o // 2, o % 2] = bucket
    for k in range(1, spots):
        to_row(k).start()
    row_local.start()

    def mask(b, carry):
        visible = jnp.zeros((count * n_pre, page_len), jnp.int32)
        page = lax.broadcasted_iota(jnp.int32, visible.shape, 0)
        token = lax.broadcasted_iota(jnp.int32, visible.shape, 1)
        for slot in range(lists_ref.shape[1]):
            shown = reach_ref[first + b] - slot * page_len
            visible = jnp.where(page == lists_ref[first + b, slot], shown, visible)
        bias = jnp.where(token < visible, 0.0, MASKED).astype(jnp.float32)
        for p in range(count * n_pre):
            bias_ref[b, :, p * page_len : (p + 1) * page_len] = bias[p : p + 1]
        return carry

    lax.fori_loop(0, branches, mask, 0)

    @pl.when(spot == 0)
    def _():
        def clear(t, carry):
            got[t] = jnp.zeros(got.shape[1:], got.dtype)
            return carry

        lax.fori_loop(0, spots, clear, 0)

    @pl.when(spot == spots - 1)
    def _():
        def clear(t, carry):
            got[t + t // (spots - 1)] = jnp.zeros(got.shape[1:], got.dtype)
            return carry

        lax.fori_loop(0, spots, clear, 0)

    pass_on(0, 0)
    for k in range(1, chips):
        across(k).wait_recv()
        beside(k).start()

    pass_on(0, 1)
    for copy in loads:
        copy.wait()
    for k in range(chips):
        beside(k).wait_recv()
    load_values(all_ref, values)

    def load_rest(step, carry):
        own_rows(step).start()
        return carry

    lax.fori_loop(1, spots, load_rest, 0)

    total = branches * blocks
    last = branches - 1

    def at(n, where):
        def run(act):
            @pl.when(n == where)
            def _():
                act()

        return run

    def first_chunks(b, carry):
        for g in range(blocks):
            attn_copy(b, g).wait_recv()
        for c in range(pieces):
            send_chunk(0, b, c)
        return carry

    def turn(n, carry):
        b = n // blocks
        g = lax.rem(n, blocks)
        start = pl.multiple_of(g * span, span)
        attend(b, start, block, q_ref, own_ref, all_ref, bias_ref, values, attn)

        @at(n, last * blocks)
        def _():
            to_mate(1, 0).start()

        attn_copy(b, g).start()

        @at(n, 0)
        def _():
            pass_on(0, 2)
            pass_over(0, 0)

        @at(n, 2)
        def _():
            pass_on(0, 3)
            pass_over(0, 1)

        @at(n, 4)
        def _():
            pass_over(0, 2)

        @at(n, 6)
        def _():
            pass_over(0, 3)
            own_rows(0).wait()
            for c in range(pieces):
                need(0, c)
            first_chunks(0, 0)

        return carry

    lax.fori_loop(0, total, turn, 0)
    for c in range(1, pieces):
        to_mate(1, c).start()
    if spots > 2:
        for c in range(pieces):
            to_mate(2, c).start()
    lax.fori_loop(1, last, first_chunks, 0)
    own_rows(1).wait()
    pass_on(1, 0)
    pass_over(1, 0)
    need(1, 0)

    def second_chunk(b, carry):
        send_chunk(1, b, 0)
        return carry

    lax.fori_loop(0, last, second_chunk, 0)
    first_chunks(last, 0)
    second_chunk(last, 0)
    pass_on(1, 1)
    pass_on(1, 2)
    pass_over(1, 1)
    pass_on(1, 3)

    def ahead(act, step, c, by):
        where = step + (c + by) // pieces

        @pl.when(where < spots)
        def _():
            act(where, (c + by) % pieces)

    def column(step, c, act):
        need(step, c)

        def over(b, carry):
            act(b, c)
            return carry

        lax.fori_loop(0, branches, over, 0)
        ahead(pass_over, step, c, 1)
        ahead(pass_on, step, c, 3)

    def phase(step, carry):
        for c in range(pieces):
            if c == 0:
                @pl.when(step > 1)
                def _():
                    own_rows(step).wait()
                    column(step, 0, functools.partial(send_chunk, step))
            else:
                column(step, c, functools.partial(send_chunk, step))
            if c == 1:
                @pl.when(step + 2 < spots)
                def _():
                    for p in range(pieces):
                        to_mate(step + 2, p).start()

                @pl.when(step == spots - 2)
                def _():
                    pages_to_side()

        return carry

    lax.fori_loop(1, spots - 1, phase, 0)
    own_rows(spots - 1).wait()
    pages_to_home()
    for c in range(pieces):
        column(spots - 1, c, last_chunk)

    def drain_attn(b, carry):
        for g in range(blocks):
            attn_copy(b, g).wait_send()
        return carry

    lax.fori_loop(0, branches, drain_attn, 0)

    def drain_weight(step, carry):
        for c in range(pieces):
            to_mate(step, c).wait_send()
            for k in range(1, chips):
                to_chip(step, c, k).wait_send()
            for k in range(chips):
                to_core(step, c, k).wait_send()
        return carry

    lax.fori_loop(0, spots, drain_weight, 0)

    def drain_chunks(step, carry):
        def over(b, inner):
            for c in range(pieces):
                chunk_copy(step, b, c).wait_send()
            return inner

        return lax.fori_loop(0, branches, over, carry)

    lax.fori_loop(0, spots - 1, drain_chunks, 0)
    for k in range(1, chips):
        across(k).wait_send()
    for k in range(chips):
        beside(k).wait_send()
    for k in range(1, spots):
        to_row(k).wait_send()
    to_side.wait_send()
    for part in range(ratio):
        home_local(part).wait()
        for k in range(1, n_pre):
            to_home(k, part).wait_send()
            to_home(k, part).wait_recv()


def settle_kernel(*refs):
    count = (len(refs) - 1) // 2
    sem = refs[-1]
    copies = [
        pltpu.make_async_copy(refs[i], refs[count + i], sem.at[i]) for i in range(count)
    ]
    for copy in copies:
        copy.start()
    for copy in copies:
        copy.wait()


def settle(*arrays):
    anywhere = pl.BlockSpec(memory_space=pl.ANY)
    return pl.pallas_call(
        settle_kernel,
        out_shape=tuple(jax.ShapeDtypeStruct(a.shape, a.dtype) for a in arrays),
        in_specs=[anywhere] * len(arrays),
        out_specs=(anywhere,) * len(arrays),
        scratch_shapes=[pltpu.SemaphoreType.DMA((len(arrays),))],
        name="settle",
    )(*arrays)


def layer(lists, reach, owner, kv, pool, queries, own, weight, n_pre, n_dec):
    branches, page_len, depth = queries.shape
    count = pool.shape[0]
    cols = weight.shape[1] // n_dec
    ratio = n_dec // n_pre
    chips = n_pre // 2
    spots = n_dec // 2
    blocks = depth // (min(BLOCK, depth // (PAIR * HD)) * PAIR * HD)
    bf16 = jnp.bfloat16
    anywhere = pl.BlockSpec(memory_space=pl.ANY)
    dma = pltpu.SemaphoreType.DMA
    return pl.pallas_call(
        functools.partial(layer_kernel, n_pre, n_dec),
        out_shape=(
            pltpu.VMEM((branches, page_len, cols), bf16),
            pltpu.VMEM((n_pre, page_len, ratio * kv.shape[2]), bf16),
        ),
        in_specs=[SMEM] * 3 + [VMEM] + [anywhere] * 4,
        out_specs=(VMEM, VMEM),
        scratch_shapes=[
            pltpu.VMEM((count * n_pre,) + pool.shape[1:], bf16),
            pltpu.VMEM(queries.shape, bf16),
            pltpu.VMEM(own.shape, bf16),
            pltpu.VMEM((count * n_pre * page_len, 2 * HD), bf16),
            pltpu.VMEM((branches, page_len, 2 * depth), bf16),
            pltpu.VMEM((spots, 2 * depth, cols), bf16),
            pltpu.VMEM((spots, branches, page_len, cols), bf16),
            pltpu.VMEM((spots + 1, branches, page_len, cols), bf16),
            pltpu.VMEM((branches, 1, count * n_pre * page_len), jnp.float32),
            pltpu.VMEM((spots, 2) + kv.shape[1:], bf16),
            pltpu.VMEM((spots, 2) + kv.shape[1:], bf16),
            pltpu.VMEM((2, spots) + kv.shape[1:], bf16),
            dma((3,)),
            dma((spots,)),
            dma((n_pre,)),
            dma((n_pre,)),
            dma((spots,)),
            dma((spots,)),
            dma((1,)),
            dma((2,)),
            dma((n_pre, ratio)),
            dma((n_pre, ratio)),
            dma((branches, blocks)),
            dma((branches, blocks)),
            dma((spots, PIECES)),
            dma((spots, PIECES)),
            dma((spots, PIECES, chips)),
            dma((spots, PIECES, chips)),
            dma((spots, PIECES, chips)),
            dma((spots, PIECES, chips)),
            dma((spots, branches, PIECES)),
            dma((spots + 1, branches, PIECES)),
        ],
        compiler_params=pltpu.CompilerParams(
            has_side_effects=True, collective_id=0, vmem_limit_bytes=62 * 2**20
        ),
        name="layer",
    )(lists, reach, owner, kv, pool, queries, own, weight)


def on_device(
    queries, branch_kv, pool_kv, page_lists, anc_len, dec_owner, output_projection_weight
):
    n_pre = lax.axis_size("pre")
    n_dec = lax.axis_size("dec")
    dec_idx = lax.axis_index("dec")
    kv_cols = pool_kv.shape[2]
    if kv_cols < 2 * HD:
        other_pool, other_own = from_partner((pool_kv, branch_kv), "dec", 0)
        first_half = dec_idx % 2 == 0
        pool = jnp.where(
            first_half,
            jnp.concatenate([pool_kv, other_pool], 2),
            jnp.concatenate([other_pool, pool_kv], 2),
        )
        own = jnp.where(
            first_half,
            jnp.concatenate([branch_kv, other_own], 2),
            jnp.concatenate([other_own, branch_kv], 2),
        )
    else:
        pool, own = pool_kv, branch_kv

    layer_out, decode_pages = layer(
        page_lists,
        anc_len,
        dec_owner,
        branch_kv,
        pool,
        queries,
        own,
        output_projection_weight,
        n_pre,
        n_dec,
    )
    return (layer_out, decode_pages)


def solution(mesh):
    in_specs = (
        P("pre", None, "dec"),
        P("pre", None, "dec"),
        P("pre", None, "dec"),
        P(),
        P(),
        P(),
        P("dec", None),
    )
    out_specs = (P("pre", None, "dec"), P("dec", None, "pre"))
    return jax.shard_map(
        on_device, mesh=mesh, in_specs=in_specs, out_specs=out_specs, check_vma=False
    )
```

```python
import functools
import math

import jax
import jax.numpy as jnp
from jax import lax
from jax.experimental import pallas as pl
from jax.experimental.pallas import tpu as pltpu
from jax.sharding import PartitionSpec as P

HD = 128
MASKED = -1e30
SCALE = HD**-0.5 * math.log2(math.e)
MESH = pl.DeviceIdType.MESH
VMEM = pl.BlockSpec(memory_space=pltpu.VMEM)
PAIR = 2
BLOCK = 2
PIECES = 4


def from_partner(value, axis, stride):
    mask = 2**stride
    pairs = [(source, source ^ mask) for source in range(lax.axis_size(axis))]
    return lax.ppermute(value, axis, pairs)


def load_values(pool_ref, values):
    pages, page_len, _ = pool_ref.shape
    values[:, :HD] = pool_ref[:, :, HD:].reshape(pages * page_len, HD)
    values[:, HD:] = jnp.ones((pages * page_len, HD), values.dtype)


def attend(branch, start, block, q_ref, own_ref, pool_ref, bias_ref, values, attn):
    pages, page_len, _ = pool_ref.shape
    keys = pool_ref[:, :, :HD].reshape(pages * page_len, HD)
    own_keys = own_ref[branch, :, :HD]
    own_values = own_ref[branch, :, HD:]
    own_values = jnp.concatenate([own_values, jnp.ones_like(own_values)], 1)
    row = lax.broadcasted_iota(jnp.int32, (page_len, page_len), 0)
    col = lax.broadcasted_iota(jnp.int32, (page_len, page_len), 1)
    causal = jnp.where(col <= row, 0.0, MASKED)
    causal = jnp.concatenate([causal] * PAIR, 0)
    bias = bias_ref[branch]
    nt = (((1,), (1,)), ((), ()))
    outs = []
    for g in range(block):
        q = q_ref[branch, :, pl.ds(start + g * PAIR * HD, PAIR * HD)]
        q = jnp.concatenate([q[:, i * HD : (i + 1) * HD] for i in range(PAIR)], 0)
        far = lax.dot_general(q, keys, nt, preferred_element_type=jnp.float32) + bias
        near = lax.dot_general(q, own_keys, nt, preferred_element_type=jnp.float32) + causal
        top = jnp.maximum(
            jnp.max(far, axis=-1, keepdims=True), jnp.max(near, axis=-1, keepdims=True)
        )
        top = top * SCALE
        far = jnp.exp2(far * SCALE - top).astype(jnp.bfloat16)
        near = jnp.exp2(near * SCALE - top).astype(jnp.bfloat16)
        out = jnp.dot(far, values[...], preferred_element_type=jnp.float32)
        out = out + jnp.dot(near, own_values, preferred_element_type=jnp.float32)
        out = (out[:, :HD] / out[:, HD:]).astype(jnp.bfloat16)
        outs.extend(out[i * page_len : (i + 1) * page_len] for i in range(PAIR))
    for i, out in enumerate(outs):
        attn[branch, :, pl.ds(start + i * HD, HD)] = out


def layer_kernel(
    n_pre,
    n_dec,
    lists_hbm,
    reach_hbm,
    owner_hbm,
    kv_hbm,
    pool_ref,
    q_hbm,
    own_hbm,
    w_ref,
    out_ref,
    pages_ref,
    all_ref,
    q_ref,
    own_ref,
    values,
    attn,
    wv,
    sent,
    got,
    bias_ref,
    bucket_ref,
    row_ref,
    block_ref,
    lists_ref,
    reach_ref,
    owner_ref,
    kv_ref,
    far_weight,
    far_sent,
    far_land,
    far_got,
    load_sem,
    wsem,
    psend,
    precv,
    bsend,
    brecv,
    msend,
    mrecv,
    hsend,
    hrecv,
    asend,
    arecv,
    ysend,
    yrecv,
    xsend,
    xrecv,
    csend,
    crecv,
    greet,
    ssem,
    rsem,
    fsend,
    frecv,
    gsem,
):
    pre = lax.axis_index("pre")
    dec = lax.axis_index("dec")
    branches, page_len, cols = out_ref.shape
    depth = w_ref.shape[0]
    count = pool_ref.shape[0]
    width = kv_ref.shape[2]
    ratio = n_dec // n_pre
    chips = n_pre // 2
    chip = pre // 2
    core = lax.rem(pre, 2)
    spots = n_dec // 2
    spot = dec // 2
    side = lax.rem(dec, 2)
    mate = dec + 1 - 2 * side
    share = depth // n_pre
    pieces = PIECES
    piece = cols // pieces
    block = min(BLOCK, depth // (PAIR * HD))
    span = block * PAIR * HD
    blocks = depth // span
    low = 2 * spot < spots
    outer = jnp.logical_or(spot == 0, spot == spots - 1)
    across_end = spots - 1 - spot

    def target(step):
        near = jnp.where(low, spot, spots - 1 - spot)
        paired = jnp.where(step % 2 == 0, spots - 1 - step // 2, step // 2)
        t = jnp.where(step < 2 * near, paired, spots - 1 - step + near)
        return jnp.where(low, t, spots - 1 - t)

    def block_of(device):
        return pl.ds(device * count, count)

    def across(k):
        return pltpu.make_async_remote_copy(
            src_ref=pool_ref,
            dst_ref=all_ref.at[block_of(pre)],
            send_sem=psend.at[k],
            recv_sem=precv.at[k],
            device_id={"pre": lax.rem(chip + k, chips) * 2 + core},
            device_id_type=MESH,
        )

    def beside(k):
        where = all_ref.at[block_of(lax.rem(chip + chips - k, chips) * 2 + core)]
        return pltpu.make_async_remote_copy(
            src_ref=pool_ref if k == 0 else where,
            dst_ref=where,
            send_sem=psend.at[chips + k],
            recv_sem=precv.at[chips + k],
            device_id={"pre": chip * 2 + 1 - core},
            device_id_type=MESH,
        )

    def own_rows(step):
        t = target(step)
        start = pl.multiple_of((2 * t + side) * cols, cols)
        return pltpu.make_async_copy(
            w_ref.at[:, pl.ds(start, cols)], wv.at[t, pl.ds(0, depth)], wsem.at[step]
        )

    def share_of(device, step, c):
        rows = pl.ds(pl.multiple_of(depth + device * share, 16), share)
        return wv.at[target(step), rows, pl.ds(pl.multiple_of(c * piece, piece), piece)]

    def to_mate(step, c):
        start = pl.multiple_of((2 * target(step) + 1 - side) * cols + c * piece, piece)
        rows = pl.ds(pl.multiple_of(pre * share, 16), share)
        return pltpu.make_async_remote_copy(
            src_ref=w_ref.at[rows, pl.ds(start, piece)],
            dst_ref=share_of(pre, step, c),
            send_sem=ysend.at[step, c],
            recv_sem=yrecv.at[step, c],
            device_id={"dec": mate},
            device_id_type=MESH,
        )

    def to_chip(step, c, k):
        return pltpu.make_async_remote_copy(
            src_ref=share_of(pre, step, c),
            dst_ref=share_of(pre, step, c),
            send_sem=xsend.at[step, c, k],
            recv_sem=xrecv.at[step, c, k],
            device_id={"pre": lax.rem(chip + k, chips) * 2 + core},
            device_id_type=MESH,
        )

    def to_core(step, c, k):
        where = share_of(lax.rem(chip + chips - k, chips) * 2 + core, step, c)
        return pltpu.make_async_remote_copy(
            src_ref=where,
            dst_ref=where,
            send_sem=csend.at[step, c, k],
            recv_sem=crecv.at[step, c, k],
            device_id={"pre": chip * 2 + 1 - core},
            device_id_type=MESH,
        )

    def pass_on(step, c):
        to_mate(step, c).wait_recv()
        for k in range(1, chips):
            to_chip(step, c, k).start()
        to_core(step, c, 0).start()

    def pass_over(step, c):
        for k in range(1, chips):
            to_chip(step, c, k).wait_recv()
            to_core(step, c, k).start()

    def need(step, c):
        for k in range(chips):
            to_core(step, c, k).wait_recv()

    def attn_copy(b, g):
        start = pl.multiple_of(g * span, span)
        return pltpu.make_async_remote_copy(
            src_ref=attn.at[b, :, pl.ds(start, span)],
            dst_ref=attn.at[b, :, pl.ds(depth + start, span)],
            send_sem=asend.at[b, g],
            recv_sem=arecv.at[b, g],
            device_id={"dec": mate},
            device_id_type=MESH,
        )

    def far_rows():
        start = pl.multiple_of((2 * across_end + 1 - side) * cols, cols)
        return pltpu.make_async_copy(
            w_ref.at[:, pl.ds(start, cols)], far_weight, load_sem.at[7]
        )

    def far_copy(c):
        return pltpu.make_async_remote_copy(
            src_ref=far_sent.at[:, at_piece(c)],
            dst_ref=far_land.at[:, at_piece(c)],
            send_sem=fsend.at[c],
            recv_sem=frecv.at[c],
            device_id={"dec": 2 * across_end + side},
            device_id_type=MESH,
        )

    def far_give():
        return pltpu.make_async_remote_copy(
            src_ref=far_land,
            dst_ref=far_got,
            send_sem=gsem.at[0],
            recv_sem=gsem.at[1],
            device_id={"dec": mate},
            device_id_type=MESH,
        )

    def at_piece(c):
        return pl.ds(pl.multiple_of(c * piece, piece), piece)

    def arrival(slot, b, c):
        where = got.at[slot, b, :, at_piece(c)]
        return pltpu.make_async_copy(where, where, rsem.at[slot, b, c])

    def chunk_copy(step, b, c):
        t = target(step)
        onward = t > spot
        slot = jnp.where(t == spot - 1, spots, t)
        return pltpu.make_async_remote_copy(
            src_ref=sent.at[t, b, :, at_piece(c)],
            dst_ref=got.at[slot, b, :, at_piece(c)],
            send_sem=ssem.at[step, b, c],
            recv_sem=rsem.at[slot, b, c],
            device_id={"dec": jnp.where(onward, dec + 2, dec - 2)},
            device_id_type=MESH,
        )

    def send_chunk(step, b, c):
        t = target(step)
        relayed = jnp.where(t > spot, spot > 0, spot < spots - 1)

        @pl.when(relayed)
        def _():
            arrival(t, b, c).wait()

        total = jnp.dot(attn[b], wv[t, :, at_piece(c)], preferred_element_type=jnp.float32)
        total = total + got[t, b, :, at_piece(c)].astype(jnp.float32)
        sent[t, b, :, at_piece(c)] = total.astype(jnp.bfloat16)
        chunk_copy(step, b, c).start()

    def last_chunk(b, c):
        @pl.when(spot > 0)
        def _():
            arrival(spot, b, c).wait()

        @pl.when(spot < spots - 1)
        def _():
            arrival(spots, b, c).wait()

        total = jnp.dot(attn[b], wv[spot, :, at_piece(c)], preferred_element_type=jnp.float32)
        total = total + got[spot, b, :, at_piece(c)].astype(jnp.float32)
        total = total + got[spots, b, :, at_piece(c)].astype(jnp.float32)
        out_ref[b, :, at_piece(c)] = total.astype(jnp.bfloat16)

        @pl.when(jnp.logical_and(outer, b == 0))
        def _():
            whole = total + far_got[:, at_piece(c)].astype(jnp.float32)
            out_ref[b, :, at_piece(c)] = whole.astype(jnp.bfloat16)

    def to_row(k):
        where = lax.rem(spot + k, spots)
        return pltpu.make_async_remote_copy(
            src_ref=bucket_ref.at[where],
            dst_ref=row_ref.at[spot],
            send_sem=bsend.at[k],
            recv_sem=brecv.at[k],
            device_id={"dec": 2 * where + side},
            device_id_type=MESH,
        )

    row_local = pltpu.make_async_copy(bucket_ref.at[spot], row_ref.at[spot], brecv.at[0])
    to_side = pltpu.make_async_remote_copy(
        src_ref=row_ref.at[:, 1 - side],
        dst_ref=block_ref.at[side],
        send_sem=msend.at[0],
        recv_sem=mrecv.at[0],
        device_id={"dec": mate},
        device_id_type=MESH,
    )
    side_local = pltpu.make_async_copy(row_ref.at[:, side], block_ref.at[side], mrecv.at[1])

    def home_parts(k, part):
        home = lax.rem(pre + k, n_pre)
        source = home * ratio + part
        src = block_ref.at[lax.rem(source, 2), source // 2]
        return home, src, pages_ref.at[pre, :, pl.ds(part * width, width)]

    def to_home(k, part):
        home, src, dst = home_parts(k, part)
        return pltpu.make_async_remote_copy(
            src_ref=src,
            dst_ref=dst,
            send_sem=hsend.at[k, part],
            recv_sem=hrecv.at[k, part],
            device_id={"pre": home},
            device_id_type=MESH,
        )

    def home_local(part):
        _, src, dst = home_parts(0, part)
        return pltpu.make_async_copy(src, dst, hrecv.at[0, part])

    def pages_to_side():
        for k in range(1, spots):
            to_row(k).wait_recv()
        row_local.wait()
        to_side.start()
        side_local.start()

    def pages_to_home():
        to_side.wait_recv()
        side_local.wait()
        for part in range(ratio):
            home_local(part).start()
            for k in range(1, n_pre):
                to_home(k, part).start()

    barrier = pltpu.get_barrier_semaphore()
    for k in range(1, n_pre):
        pl.semaphore_signal(
            barrier, 1, device_id={"pre": lax.rem(pre + k, n_pre)}, device_id_type=MESH
        )
    pl.semaphore_signal(barrier, 1, device_id={"dec": mate}, device_id_type=MESH)
    def signal_along(above, below):
        @pl.when(spot < spots - 1)
        def _():
            pl.semaphore_signal(above, 1, device_id={"dec": dec + 2}, device_id_type=MESH)

        @pl.when(spot > 0)
        def _():
            pl.semaphore_signal(below, 1, device_id={"dec": dec - 2}, device_id_type=MESH)

    def greet_further():
        for k in range(spots - 2):
            signal_along(greet.at[0, k], greet.at[1, k])

            @pl.when(spot > 0)
            def _(k=k):
                pl.semaphore_wait(greet.at[0, k], 1)

            @pl.when(spot < spots - 1)
            def _(k=k):
                pl.semaphore_wait(greet.at[1, k], 1)

    signal_along(barrier, barrier)
    loads = [
        pltpu.make_async_copy(pool_ref, all_ref.at[block_of(pre)], load_sem.at[0]),
        pltpu.make_async_copy(q_hbm, q_ref, load_sem.at[1]),
        pltpu.make_async_copy(own_hbm, own_ref, load_sem.at[2]),
    ]
    tables = [
        pltpu.make_async_copy(owner_hbm, owner_ref, load_sem.at[3]),
        pltpu.make_async_copy(kv_hbm, kv_ref, load_sem.at[4]),
        pltpu.make_async_copy(lists_hbm, lists_ref, load_sem.at[5]),
        pltpu.make_async_copy(reach_hbm, reach_ref, load_sem.at[6]),
    ]
    for copy in tables + loads:
        copy.start()
    own_rows(0).start()

    @pl.when(outer)
    def _():
        far_rows().start()

    pl.semaphore_wait(barrier, n_pre + jnp.minimum(spot, 1) + jnp.minimum(spots - 1 - spot, 1))

    for k in range(1, chips):
        across(k).start()
    beside(0).start()
    for c in range(pieces):
        to_mate(0, c).start()
    to_mate(1, 0).start()
    for copy in tables:
        copy.wait()
    first = pre * branches
    for o in range(n_dec):
        bucket = jnp.zeros(kv_ref.shape[1:], kv_ref.dtype)
        for b in range(branches):
            bucket = jnp.where(owner_ref[first + b] == o, kv_ref[b], bucket)
        bucket_ref[o // 2, o % 2] = bucket
    greet_further()
    for k in range(1, spots):
        to_row(k).start()
    row_local.start()

    def mask(b, carry):
        visible = jnp.zeros((count * n_pre, page_len), jnp.int32)
        page = lax.broadcasted_iota(jnp.int32, visible.shape, 0)
        token = lax.broadcasted_iota(jnp.int32, visible.shape, 1)
        for slot in range(lists_ref.shape[1]):
            shown = reach_ref[first + b] - slot * page_len
            visible = jnp.where(page == lists_ref[first + b, slot], shown, visible)
        bias = jnp.where(token < visible, 0.0, MASKED).astype(jnp.float32)
        for p in range(count * n_pre):
            bias_ref[b, :, p * page_len : (p + 1) * page_len] = bias[p : p + 1]
        return carry

    lax.fori_loop(0, branches, mask, 0)

    @pl.when(spot == 0)
    def _():
        def clear(t, carry):
            got[t] = jnp.zeros(got.shape[1:], got.dtype)
            return carry

        lax.fori_loop(0, spots, clear, 0)

    @pl.when(spot == spots - 1)
    def _():
        def clear(t, carry):
            got[t + t // (spots - 1)] = jnp.zeros(got.shape[1:], got.dtype)
            return carry

        lax.fori_loop(0, spots, clear, 0)

    pass_on(0, 0)
    for k in range(1, chips):
        across(k).wait_recv()
        beside(k).start()

    pass_on(0, 1)
    for copy in loads:
        copy.wait()
    for k in range(chips):
        beside(k).wait_recv()
    load_values(all_ref, values)

    def load_rest(step, carry):
        own_rows(step).start()
        return carry

    lax.fori_loop(1, spots, load_rest, 0)

    total = branches * blocks

    def at(n, where):
        def run(act):
            @pl.when(n == where)
            def _():
                act()

        return run

    def gathered(b):
        for g in range(blocks):
            attn_copy(b, g).wait_recv()

    def first_chunks(b, carry):
        gathered(b)
        for c in range(pieces):
            send_chunk(0, b, c)
        return carry

    def second_chunk(b, carry):
        send_chunk(1, b, 0)
        return carry

    def own_chunks():
        mine = attn[0, :, :depth]
        t = target(0)
        for c in range(pieces):
            near = jnp.dot(mine, wv[t, :depth, at_piece(c)], preferred_element_type=jnp.float32)
            sent[t, 0, :, at_piece(c)] = near.astype(jnp.bfloat16)
            chunk_copy(0, 0, c).start()
        far_rows().wait()
        for c in range(pieces):
            far = jnp.dot(mine, far_weight[:, at_piece(c)], preferred_element_type=jnp.float32)
            far_sent[:, at_piece(c)] = far.astype(jnp.bfloat16)
            far_copy(c).start()

    def turn(n, carry):
        b = n // blocks
        g = lax.rem(n, blocks)
        start = pl.multiple_of(g * span, span)
        attend(b, start, block, q_ref, own_ref, all_ref, bias_ref, values, attn)

        @pl.when(b > 0)
        def _():
            attn_copy(b, g).start()

        @at(n, blocks - 1)
        def _():
            own_rows(0).wait()

            @pl.when(outer)
            def _():
                own_chunks()

        @at(n, 0)
        def _():
            pass_on(0, 2)
            pass_over(0, 0)

        @at(n, 2)
        def _():
            pass_on(0, 3)
            pass_over(0, 1)

        @at(n, 3)
        def _():
            pass_on(1, 0)

        @at(n, 4)
        def _():
            pass_over(0, 2)

        @at(n, 5)
        def _():
            pass_over(0, 3)

        @at(n, 6)
        def _():
            pass_over(1, 0)

        return carry

    lax.fori_loop(0, total, turn, 0)
    to_mate(1, 1).start()
    for g in range(blocks):
        attn_copy(0, g).start()
    for c in range(2, pieces):
        to_mate(1, c).start()
    if spots > 2:
        for c in range(pieces):
            to_mate(2, c).start()
    for c in range(pieces):
        need(0, c)
    lax.fori_loop(1, branches, first_chunks, 0)
    own_rows(1).wait()
    need(1, 0)
    lax.fori_loop(1, branches, second_chunk, 0)
    pass_on(1, 1)
    pass_over(1, 1)

    @pl.when(outer)
    def _():
        gathered(0)

    @pl.when(jnp.logical_not(outer))
    def _():
        first_chunks(0, 0)

    second_chunk(0, 0)
    pass_on(1, 2)

    def ahead(act, step, c, by):
        where = step + (c + by) // pieces

        @pl.when(where < spots)
        def _():
            act(where, (c + by) % pieces)

    def column(step, c, act):
        need(step, c)

        def over(b, carry):
            act(b, c)
            return carry

        lax.fori_loop(0, branches, over, 0)
        if c == 1:
            @pl.when(step == 1)
            def _():
                pass_on(1, 3)

        ahead(pass_over, step, c, 1)
        ahead(pass_on, step, c, 3)

    def phase(step, carry):
        for c in range(pieces):
            if c == 0:
                @pl.when(step > 1)
                def _():
                    own_rows(step).wait()
                    column(step, 0, functools.partial(send_chunk, step))
            else:
                column(step, c, functools.partial(send_chunk, step))
            if c == 1:
                @pl.when(step + 2 < spots)
                def _():
                    for p in range(pieces):
                        to_mate(step + 2, p).start()

                @pl.when(step == spots - 2)
                def _():
                    @pl.when(outer)
                    def _():
                        for p in range(pieces):
                            far_copy(p).wait_recv()
                        far_give().start()

                    pages_to_side()

        return carry

    lax.fori_loop(1, spots - 1, phase, 0)
    own_rows(spots - 1).wait()

    @pl.when(outer)
    def _():
        far_give().wait_recv()

    for c in range(pieces):
        column(spots - 1, c, last_chunk)
        if c == 0:
            pages_to_home()

    @pl.when(outer)
    def _():
        far_give().wait_send()
        for c in range(pieces):
            far_copy(c).wait_send()


    def drain_attn(b, carry):
        for g in range(blocks):
            attn_copy(b, g).wait_send()
        return carry

    lax.fori_loop(0, branches, drain_attn, 0)

    def drain_weight(step, carry):
        for c in range(pieces):
            to_mate(step, c).wait_send()
            for k in range(1, chips):
                to_chip(step, c, k).wait_send()
            for k in range(chips):
                to_core(step, c, k).wait_send()
        return carry

    lax.fori_loop(0, spots, drain_weight, 0)

    def drain_chunks(step, carry):
        def over(b, inner):
            for c in range(pieces):
                chunk_copy(step, b, c).wait_send()
            return inner

        return lax.fori_loop(0, branches, over, carry)

    lax.fori_loop(0, spots - 1, drain_chunks, 0)
    for k in range(1, chips):
        across(k).wait_send()
    for k in range(chips):
        beside(k).wait_send()
    for k in range(1, spots):
        to_row(k).wait_send()
    to_side.wait_send()
    for part in range(ratio):
        home_local(part).wait()
        for k in range(1, n_pre):
            to_home(k, part).wait_send()
            to_home(k, part).wait_recv()


def settle_kernel(*refs):
    count = (len(refs) - 1) // 2
    sem = refs[-1]
    copies = [
        pltpu.make_async_copy(refs[i], refs[count + i], sem.at[i]) for i in range(count)
    ]
    for copy in copies:
        copy.start()
    for copy in copies:
        copy.wait()


def settle(*arrays):
    anywhere = pl.BlockSpec(memory_space=pl.ANY)
    return pl.pallas_call(
        settle_kernel,
        out_shape=tuple(jax.ShapeDtypeStruct(a.shape, a.dtype) for a in arrays),
        in_specs=[anywhere] * len(arrays),
        out_specs=(anywhere,) * len(arrays),
        scratch_shapes=[pltpu.SemaphoreType.DMA((len(arrays),))],
        name="settle",
    )(*arrays)


def layer(lists, reach, owner, kv, pool, queries, own, weight, n_pre, n_dec):
    branches, page_len, depth = queries.shape
    count = pool.shape[0]
    cols = weight.shape[1] // n_dec
    ratio = n_dec // n_pre
    chips = n_pre // 2
    spots = n_dec // 2
    blocks = depth // (min(BLOCK, depth // (PAIR * HD)) * PAIR * HD)
    bf16 = jnp.bfloat16
    anywhere = pl.BlockSpec(memory_space=pl.ANY)
    dma = pltpu.SemaphoreType.DMA
    return pl.pallas_call(
        functools.partial(layer_kernel, n_pre, n_dec),
        out_shape=(
            pltpu.VMEM((branches, page_len, cols), bf16),
            pltpu.VMEM((n_pre, page_len, ratio * kv.shape[2]), bf16),
        ),
        in_specs=[anywhere] * 8,
        out_specs=(VMEM, VMEM),
        scratch_shapes=[
            pltpu.VMEM((count * n_pre,) + pool.shape[1:], bf16),
            pltpu.VMEM(queries.shape, bf16),
            pltpu.VMEM(own.shape, bf16),
            pltpu.VMEM((count * n_pre * page_len, 2 * HD), bf16),
            pltpu.VMEM((branches, page_len, 2 * depth), bf16),
            pltpu.VMEM((spots, 2 * depth, cols), bf16),
            pltpu.VMEM((spots, branches, page_len, cols), bf16),
            pltpu.VMEM((spots + 1, branches, page_len, cols), bf16),
            pltpu.VMEM((branches, 1, count * n_pre * page_len), jnp.float32),
            pltpu.VMEM((spots, 2) + kv.shape[1:], bf16),
            pltpu.VMEM((spots, 2) + kv.shape[1:], bf16),
            pltpu.VMEM((2, spots) + kv.shape[1:], bf16),
            pltpu.SMEM(lists.shape, jnp.int32),
            pltpu.SMEM(reach.shape, jnp.int32),
            pltpu.SMEM(owner.shape, jnp.int32),
            pltpu.VMEM(kv.shape, bf16),
            pltpu.VMEM((depth, cols), bf16),
            pltpu.VMEM((page_len, cols), bf16),
            pltpu.VMEM((page_len, cols), bf16),
            pltpu.VMEM((page_len, cols), bf16),
            dma((8,)),
            dma((spots,)),
            dma((n_pre,)),
            dma((n_pre,)),
            dma((spots,)),
            dma((spots,)),
            dma((1,)),
            dma((2,)),
            dma((n_pre, ratio)),
            dma((n_pre, ratio)),
            dma((branches, blocks)),
            dma((branches, blocks)),
            dma((spots, PIECES)),
            dma((spots, PIECES)),
            dma((spots, PIECES, chips)),
            dma((spots, PIECES, chips)),
            dma((spots, PIECES, chips)),
            dma((spots, PIECES, chips)),
            pltpu.SemaphoreType.REGULAR((2, spots - 2)),
            dma((spots, branches, PIECES)),
            dma((spots + 1, branches, PIECES)),
            dma((PIECES,)),
            dma((PIECES,)),
            dma((2,)),
        ],
        compiler_params=pltpu.CompilerParams(
            has_side_effects=True, collective_id=0, vmem_limit_bytes=62 * 2**20
        ),
        name="layer",
    )(lists, reach, owner, kv, pool, queries, own, weight)


def on_device(
    queries, branch_kv, pool_kv, page_lists, anc_len, dec_owner, output_projection_weight
):
    n_pre = lax.axis_size("pre")
    n_dec = lax.axis_size("dec")
    dec_idx = lax.axis_index("dec")
    kv_cols = pool_kv.shape[2]
    if kv_cols < 2 * HD:
        other_pool, other_own = from_partner((pool_kv, branch_kv), "dec", 0)
        first_half = dec_idx % 2 == 0
        pool = jnp.where(
            first_half,
            jnp.concatenate([pool_kv, other_pool], 2),
            jnp.concatenate([other_pool, pool_kv], 2),
        )
        own = jnp.where(
            first_half,
            jnp.concatenate([branch_kv, other_own], 2),
            jnp.concatenate([other_own, branch_kv], 2),
        )
    else:
        pool, own = pool_kv, branch_kv

    layer_out, decode_pages = layer(
        page_lists,
        anc_len,
        dec_owner,
        branch_kv,
        pool,
        queries,
        own,
        output_projection_weight,
        n_pre,
        n_dec,
    )
    return (layer_out, decode_pages)


def solution(mesh):
    in_specs = (
        P("pre", None, "dec"),
        P("pre", None, "dec"),
        P("pre", None, "dec"),
        P(),
        P(),
        P(),
        P("dec", None),
    )
    out_specs = (P("pre", None, "dec"), P("dec", None, "pre"))
    return jax.shard_map(
        on_device, mesh=mesh, in_specs=in_specs, out_specs=out_specs, check_vma=False
    )
```

```python
import functools
import math

import jax
import jax.numpy as jnp
from jax import lax
from jax.experimental import pallas as pl
from jax.experimental.pallas import tpu as pltpu
from jax.sharding import PartitionSpec as P

HD = 128
MASKED = -1e30
SCALE = HD**-0.5 * math.log2(math.e)
MESH = pl.DeviceIdType.MESH
VMEM = pl.BlockSpec(memory_space=pltpu.VMEM)
PAIR = 2
BLOCK = 2
PIECES = 4


def from_partner(value, axis, stride):
    mask = 2**stride
    pairs = [(source, source ^ mask) for source in range(lax.axis_size(axis))]
    return lax.ppermute(value, axis, pairs)


def load_values(pool_ref, values):
    pages, page_len, _ = pool_ref.shape
    values[:, :HD] = pool_ref[:, :, HD:].reshape(pages * page_len, HD)
    values[:, HD:] = jnp.ones((pages * page_len, HD), values.dtype)


def attend(branch, start, block, q_ref, own_ref, pool_ref, bias_ref, values, attn):
    pages, page_len, _ = pool_ref.shape
    keys = pool_ref[:, :, :HD].reshape(pages * page_len, HD)
    own_keys = own_ref[branch, :, :HD]
    own_values = own_ref[branch, :, HD:]
    own_values = jnp.concatenate([own_values, jnp.ones_like(own_values)], 1)
    row = lax.broadcasted_iota(jnp.int32, (page_len, page_len), 0)
    col = lax.broadcasted_iota(jnp.int32, (page_len, page_len), 1)
    causal = jnp.where(col <= row, 0.0, MASKED)
    causal = jnp.concatenate([causal] * PAIR, 0)
    bias = bias_ref[branch]
    nt = (((1,), (1,)), ((), ()))
    outs = []
    for g in range(block):
        q = q_ref[branch, :, pl.ds(start + g * PAIR * HD, PAIR * HD)]
        q = jnp.concatenate([q[:, i * HD : (i + 1) * HD] for i in range(PAIR)], 0)
        far = lax.dot_general(q, keys, nt, preferred_element_type=jnp.float32) + bias
        near = lax.dot_general(q, own_keys, nt, preferred_element_type=jnp.float32) + causal
        top = jnp.maximum(
            jnp.max(far, axis=-1, keepdims=True), jnp.max(near, axis=-1, keepdims=True)
        )
        top = top * SCALE
        far = jnp.exp2(far * SCALE - top).astype(jnp.bfloat16)
        near = jnp.exp2(near * SCALE - top).astype(jnp.bfloat16)
        out = jnp.dot(far, values[...], preferred_element_type=jnp.float32)
        out = out + jnp.dot(near, own_values, preferred_element_type=jnp.float32)
        out = (out[:, :HD] / out[:, HD:]).astype(jnp.bfloat16)
        outs.extend(out[i * page_len : (i + 1) * page_len] for i in range(PAIR))
    for i, out in enumerate(outs):
        attn[branch, :, pl.ds(start + i * HD, HD)] = out


def layer_kernel(
    n_pre,
    n_dec,
    lists_hbm,
    reach_hbm,
    owner_hbm,
    kv_hbm,
    pool_ref,
    q_hbm,
    own_hbm,
    w_ref,
    out_ref,
    pages_ref,
    all_ref,
    q_ref,
    own_ref,
    values,
    attn,
    wv,
    sent,
    got,
    bias_ref,
    bucket_ref,
    row_ref,
    block_ref,
    lists_ref,
    reach_ref,
    owner_ref,
    kv_ref,
    far_weight,
    far_sent,
    far_land,
    far_got,
    load_sem,
    wsem,
    psend,
    precv,
    bsend,
    brecv,
    msend,
    mrecv,
    hsend,
    hrecv,
    asend,
    arecv,
    ysend,
    yrecv,
    xsend,
    xrecv,
    csend,
    crecv,
    greet,
    ssem,
    rsem,
    fsend,
    frecv,
    gsem,
):
    pre = lax.axis_index("pre")
    dec = lax.axis_index("dec")
    branches, page_len, cols = out_ref.shape
    depth = w_ref.shape[0]
    count = pool_ref.shape[0]
    width = kv_ref.shape[2]
    ratio = n_dec // n_pre
    chips = n_pre // 2
    chip = pre // 2
    core = lax.rem(pre, 2)
    spots = n_dec // 2
    spot = dec // 2
    side = lax.rem(dec, 2)
    mate = dec + 1 - 2 * side
    share = depth // n_pre
    pieces = PIECES
    piece = cols // pieces
    block = min(BLOCK, depth // (PAIR * HD))
    span = block * PAIR * HD
    blocks = depth // span
    low = 2 * spot < spots
    outer = jnp.logical_or(spot == 0, spot == spots - 1)
    across_end = spots - 1 - spot

    def target(step):
        near = jnp.where(low, spot, spots - 1 - spot)
        paired = jnp.where(step % 2 == 0, spots - 1 - step // 2, step // 2)
        t = jnp.where(step < 2 * near, paired, spots - 1 - step + near)
        return jnp.where(low, t, spots - 1 - t)

    def block_of(device):
        return pl.ds(device * count, count)

    def across(k):
        return pltpu.make_async_remote_copy(
            src_ref=pool_ref,
            dst_ref=all_ref.at[block_of(pre)],
            send_sem=psend.at[k],
            recv_sem=precv.at[k],
            device_id={"pre": lax.rem(chip + k, chips) * 2 + core},
            device_id_type=MESH,
        )

    def beside(k):
        where = all_ref.at[block_of(lax.rem(chip + chips - k, chips) * 2 + core)]
        return pltpu.make_async_remote_copy(
            src_ref=pool_ref if k == 0 else where,
            dst_ref=where,
            send_sem=psend.at[chips + k],
            recv_sem=precv.at[chips + k],
            device_id={"pre": chip * 2 + 1 - core},
            device_id_type=MESH,
        )

    def own_rows(step):
        t = target(step)
        start = pl.multiple_of((2 * t + side) * cols, cols)
        return pltpu.make_async_copy(
            w_ref.at[:, pl.ds(start, cols)], wv.at[t, pl.ds(0, depth)], wsem.at[step]
        )

    def share_of(device, step, c):
        rows = pl.ds(pl.multiple_of(depth + device * share, 16), share)
        return wv.at[target(step), rows, pl.ds(pl.multiple_of(c * piece, piece), piece)]

    def to_mate(step, c):
        start = pl.multiple_of((2 * target(step) + 1 - side) * cols + c * piece, piece)
        rows = pl.ds(pl.multiple_of(pre * share, 16), share)
        return pltpu.make_async_remote_copy(
            src_ref=w_ref.at[rows, pl.ds(start, piece)],
            dst_ref=share_of(pre, step, c),
            send_sem=ysend.at[step, c],
            recv_sem=yrecv.at[step, c],
            device_id={"dec": mate},
            device_id_type=MESH,
        )

    def to_chip(step, c, k):
        return pltpu.make_async_remote_copy(
            src_ref=share_of(pre, step, c),
            dst_ref=share_of(pre, step, c),
            send_sem=xsend.at[step, c, k],
            recv_sem=xrecv.at[step, c, k],
            device_id={"pre": lax.rem(chip + k, chips) * 2 + core},
            device_id_type=MESH,
        )

    def to_core(step, c, k):
        where = share_of(lax.rem(chip + chips - k, chips) * 2 + core, step, c)
        return pltpu.make_async_remote_copy(
            src_ref=where,
            dst_ref=where,
            send_sem=csend.at[step, c, k],
            recv_sem=crecv.at[step, c, k],
            device_id={"pre": chip * 2 + 1 - core},
            device_id_type=MESH,
        )

    def pass_on(step, c):
        to_mate(step, c).wait_recv()
        for k in range(1, chips):
            to_chip(step, c, k).start()
        to_core(step, c, 0).start()

    def pass_over(step, c):
        for k in range(1, chips):
            to_chip(step, c, k).wait_recv()
            to_core(step, c, k).start()

    def need(step, c):
        for k in range(chips):
            to_core(step, c, k).wait_recv()

    def attn_copy(b, g):
        start = pl.multiple_of(g * span, span)
        return pltpu.make_async_remote_copy(
            src_ref=attn.at[b, :, pl.ds(start, span)],
            dst_ref=attn.at[b, :, pl.ds(depth + start, span)],
            send_sem=asend.at[b, g],
            recv_sem=arecv.at[b, g],
            device_id={"dec": mate},
            device_id_type=MESH,
        )

    def far_rows():
        start = pl.multiple_of((2 * across_end + 1 - side) * cols, cols)
        return pltpu.make_async_copy(
            w_ref.at[:, pl.ds(start, cols)], far_weight, load_sem.at[7]
        )

    def far_copy(c):
        return pltpu.make_async_remote_copy(
            src_ref=far_sent.at[:, at_piece(c)],
            dst_ref=far_land.at[:, at_piece(c)],
            send_sem=fsend.at[c],
            recv_sem=frecv.at[c],
            device_id={"dec": 2 * across_end + side},
            device_id_type=MESH,
        )

    def far_give():
        return pltpu.make_async_remote_copy(
            src_ref=far_land,
            dst_ref=far_got,
            send_sem=gsem.at[0],
            recv_sem=gsem.at[1],
            device_id={"dec": mate},
            device_id_type=MESH,
        )

    def at_piece(c):
        return pl.ds(pl.multiple_of(c * piece, piece), piece)

    def arrival(slot, b, c):
        where = got.at[slot, b, :, at_piece(c)]
        return pltpu.make_async_copy(where, where, rsem.at[slot, b, c])

    def chunk_copy(step, b, c):
        t = target(step)
        onward = t > spot
        slot = jnp.where(t == spot - 1, spots, t)
        return pltpu.make_async_remote_copy(
            src_ref=sent.at[t, b, :, at_piece(c)],
            dst_ref=got.at[slot, b, :, at_piece(c)],
            send_sem=ssem.at[step, b, c],
            recv_sem=rsem.at[slot, b, c],
            device_id={"dec": jnp.where(onward, dec + 2, dec - 2)},
            device_id_type=MESH,
        )

    def send_chunk(step, b, c):
        t = target(step)
        relayed = jnp.where(t > spot, spot > 0, spot < spots - 1)

        @pl.when(relayed)
        def _():
            arrival(t, b, c).wait()

        total = jnp.dot(attn[b], wv[t, :, at_piece(c)], preferred_element_type=jnp.float32)
        total = total + got[t, b, :, at_piece(c)].astype(jnp.float32)
        sent[t, b, :, at_piece(c)] = total.astype(jnp.bfloat16)
        chunk_copy(step, b, c).start()

    def last_chunk(b, c):
        @pl.when(spot > 0)
        def _():
            arrival(spot, b, c).wait()

        @pl.when(spot < spots - 1)
        def _():
            arrival(spots, b, c).wait()

        total = jnp.dot(attn[b], wv[spot, :, at_piece(c)], preferred_element_type=jnp.float32)
        total = total + got[spot, b, :, at_piece(c)].astype(jnp.float32)
        total = total + got[spots, b, :, at_piece(c)].astype(jnp.float32)
        out_ref[b, :, at_piece(c)] = total.astype(jnp.bfloat16)

        @pl.when(jnp.logical_and(outer, b == 0))
        def _():
            whole = total + far_got[:, at_piece(c)].astype(jnp.float32)
            out_ref[b, :, at_piece(c)] = whole.astype(jnp.bfloat16)

    def to_row(k):
        where = lax.rem(spot + k, spots)
        return pltpu.make_async_remote_copy(
            src_ref=bucket_ref.at[where],
            dst_ref=row_ref.at[spot],
            send_sem=bsend.at[k],
            recv_sem=brecv.at[k],
            device_id={"dec": 2 * where + side},
            device_id_type=MESH,
        )

    row_local = pltpu.make_async_copy(bucket_ref.at[spot], row_ref.at[spot], brecv.at[0])
    to_side = pltpu.make_async_remote_copy(
        src_ref=row_ref.at[:, 1 - side],
        dst_ref=block_ref.at[side],
        send_sem=msend.at[0],
        recv_sem=mrecv.at[0],
        device_id={"dec": mate},
        device_id_type=MESH,
    )
    side_local = pltpu.make_async_copy(row_ref.at[:, side], block_ref.at[side], mrecv.at[1])

    def home_parts(k, part):
        home = lax.rem(pre + k, n_pre)
        source = home * ratio + part
        src = block_ref.at[lax.rem(source, 2), source // 2]
        return home, src, pages_ref.at[pre, :, pl.ds(part * width, width)]

    def to_home(k, part):
        home, src, dst = home_parts(k, part)
        return pltpu.make_async_remote_copy(
            src_ref=src,
            dst_ref=dst,
            send_sem=hsend.at[k, part],
            recv_sem=hrecv.at[k, part],
            device_id={"pre": home},
            device_id_type=MESH,
        )

    def home_local(part):
        _, src, dst = home_parts(0, part)
        return pltpu.make_async_copy(src, dst, hrecv.at[0, part])

    def homeward(near):
        for part in range(ratio):
            for k in range(n_pre):
                source = lax.rem(pre + k, n_pre) * ratio + part
                mine = lax.rem(source, 2) == side

                @pl.when(mine if near else jnp.logical_not(mine))
                def _(k=k, part=part):
                    if k == 0:
                        home_local(part).start()
                    else:
                        to_home(k, part).start()

    def pages_to_side():
        for k in range(1, spots):
            to_row(k).wait_recv()
        row_local.wait()
        to_side.start()
        side_local.start()
        side_local.wait()
        homeward(True)

    def pages_to_home():
        to_side.wait_recv()
        homeward(False)

    barrier = pltpu.get_barrier_semaphore()
    for k in range(1, n_pre):
        pl.semaphore_signal(
            barrier, 1, device_id={"pre": lax.rem(pre + k, n_pre)}, device_id_type=MESH
        )
    pl.semaphore_signal(barrier, 1, device_id={"dec": mate}, device_id_type=MESH)
    def signal_along(above, below):
        @pl.when(spot < spots - 1)
        def _():
            pl.semaphore_signal(above, 1, device_id={"dec": dec + 2}, device_id_type=MESH)

        @pl.when(spot > 0)
        def _():
            pl.semaphore_signal(below, 1, device_id={"dec": dec - 2}, device_id_type=MESH)

    def greet_further():
        for k in range(spots - 2):
            signal_along(greet.at[0, k], greet.at[1, k])

            @pl.when(spot > 0)
            def _(k=k):
                pl.semaphore_wait(greet.at[0, k], 1)

            @pl.when(spot < spots - 1)
            def _(k=k):
                pl.semaphore_wait(greet.at[1, k], 1)

    signal_along(barrier, barrier)
    loads = [
        pltpu.make_async_copy(pool_ref, all_ref.at[block_of(pre)], load_sem.at[0]),
        pltpu.make_async_copy(q_hbm, q_ref, load_sem.at[1]),
        pltpu.make_async_copy(own_hbm, own_ref, load_sem.at[2]),
    ]
    tables = [
        pltpu.make_async_copy(owner_hbm, owner_ref, load_sem.at[3]),
        pltpu.make_async_copy(kv_hbm, kv_ref, load_sem.at[4]),
        pltpu.make_async_copy(lists_hbm, lists_ref, load_sem.at[5]),
        pltpu.make_async_copy(reach_hbm, reach_ref, load_sem.at[6]),
    ]
    for copy in tables + loads:
        copy.start()
    own_rows(0).start()

    @pl.when(outer)
    def _():
        far_rows().start()

    pl.semaphore_wait(barrier, n_pre + jnp.minimum(spot, 1) + jnp.minimum(spots - 1 - spot, 1))

    for k in range(1, chips):
        across(k).start()
    beside(0).start()
    for c in range(pieces):
        to_mate(0, c).start()
    to_mate(1, 0).start()
    for copy in tables:
        copy.wait()
    first = pre * branches
    for o in range(n_dec):
        bucket = jnp.zeros(kv_ref.shape[1:], kv_ref.dtype)
        for b in range(branches):
            bucket = jnp.where(owner_ref[first + b] == o, kv_ref[b], bucket)
        bucket_ref[o // 2, o % 2] = bucket
    greet_further()
    for k in range(1, spots):
        to_row(k).start()
    row_local.start()

    def mask(b, carry):
        visible = jnp.zeros((count * n_pre, page_len), jnp.int32)
        page = lax.broadcasted_iota(jnp.int32, visible.shape, 0)
        token = lax.broadcasted_iota(jnp.int32, visible.shape, 1)
        for slot in range(lists_ref.shape[1]):
            shown = reach_ref[first + b] - slot * page_len
            visible = jnp.where(page == lists_ref[first + b, slot], shown, visible)
        bias = jnp.where(token < visible, 0.0, MASKED).astype(jnp.float32)
        for p in range(count * n_pre):
            bias_ref[b, :, p * page_len : (p + 1) * page_len] = bias[p : p + 1]
        return carry

    lax.fori_loop(0, branches, mask, 0)

    @pl.when(spot == 0)
    def _():
        def clear(t, carry):
            got[t] = jnp.zeros(got.shape[1:], got.dtype)
            return carry

        lax.fori_loop(0, spots, clear, 0)

    @pl.when(spot == spots - 1)
    def _():
        def clear(t, carry):
            got[t + t // (spots - 1)] = jnp.zeros(got.shape[1:], got.dtype)
            return carry

        lax.fori_loop(0, spots, clear, 0)

    pass_on(0, 0)
    for k in range(1, chips):
        across(k).wait_recv()
        beside(k).start()

    pass_on(0, 1)
    for copy in loads:
        copy.wait()
    for k in range(chips):
        beside(k).wait_recv()
    load_values(all_ref, values)

    def load_rest(step, carry):
        own_rows(step).start()
        return carry

    lax.fori_loop(1, spots, load_rest, 0)

    total = branches * blocks

    def at(n, where):
        def run(act):
            @pl.when(n == where)
            def _():
                act()

        return run

    def gathered(b):
        for g in range(blocks):
            attn_copy(b, g).wait_recv()

    def first_chunks(b, carry):
        gathered(b)
        for c in range(pieces):
            send_chunk(0, b, c)
        return carry

    def second_chunk(b, carry):
        send_chunk(1, b, 0)
        return carry

    def own_chunks():
        mine = attn[0, :, :depth]
        t = target(0)
        for c in range(pieces):
            near = jnp.dot(mine, wv[t, :depth, at_piece(c)], preferred_element_type=jnp.float32)
            sent[t, 0, :, at_piece(c)] = near.astype(jnp.bfloat16)
            chunk_copy(0, 0, c).start()
        far_rows().wait()
        for c in range(pieces):
            far = jnp.dot(mine, far_weight[:, at_piece(c)], preferred_element_type=jnp.float32)
            far_sent[:, at_piece(c)] = far.astype(jnp.bfloat16)
            far_copy(c).start()

    def turn(n, carry):
        b = n // blocks
        g = lax.rem(n, blocks)
        start = pl.multiple_of(g * span, span)
        attend(b, start, block, q_ref, own_ref, all_ref, bias_ref, values, attn)

        @pl.when(b > 0)
        def _():
            attn_copy(b, g).start()

        @at(n, blocks - 1)
        def _():
            own_rows(0).wait()

            @pl.when(outer)
            def _():
                own_chunks()

        @at(n, 0)
        def _():
            pass_on(0, 2)
            pass_over(0, 0)

        @at(n, 2)
        def _():
            pass_on(0, 3)
            pass_over(0, 1)

        @at(n, 3)
        def _():
            pass_on(1, 0)

        @at(n, 4)
        def _():
            pass_over(0, 2)

        @at(n, 5)
        def _():
            pass_over(0, 3)

        @at(n, 6)
        def _():
            pass_over(1, 0)

        return carry

    lax.fori_loop(0, total, turn, 0)
    to_mate(1, 1).start()
    for g in range(blocks):
        attn_copy(0, g).start()
    for c in range(2, pieces):
        to_mate(1, c).start()
    if spots > 2:
        for c in range(pieces):
            to_mate(2, c).start()
    for c in range(pieces):
        need(0, c)
    lax.fori_loop(1, branches, first_chunks, 0)
    own_rows(1).wait()
    need(1, 0)
    lax.fori_loop(1, branches, second_chunk, 0)
    pass_on(1, 1)
    pass_over(1, 1)

    @pl.when(outer)
    def _():
        gathered(0)

    @pl.when(jnp.logical_not(outer))
    def _():
        first_chunks(0, 0)

    second_chunk(0, 0)
    pass_on(1, 2)

    def ahead(act, step, c, by):
        where = step + (c + by) // pieces

        @pl.when(where < spots)
        def _():
            act(where, (c + by) % pieces)

    def column(step, c, act):
        need(step, c)

        def over(b, carry):
            act(b, c)
            return carry

        lax.fori_loop(0, branches, over, 0)
        if c == 1:
            @pl.when(step == 1)
            def _():
                pass_on(1, 3)

        ahead(pass_over, step, c, 1)
        ahead(pass_on, step, c, 3)

    def phase(step, carry):
        for c in range(pieces):
            if c == 0:
                @pl.when(step > 1)
                def _():
                    own_rows(step).wait()
                    column(step, 0, functools.partial(send_chunk, step))
            else:
                column(step, c, functools.partial(send_chunk, step))
            if c == 1:
                @pl.when(step + 2 < spots)
                def _():
                    for p in range(pieces):
                        to_mate(step + 2, p).start()

                @pl.when(step == spots - 2)
                def _():
                    @pl.when(outer)
                    def _():
                        for p in range(pieces):
                            far_copy(p).wait_recv()
                        far_give().start()

                    pages_to_side()

        return carry

    lax.fori_loop(1, spots - 1, phase, 0)
    own_rows(spots - 1).wait()

    @pl.when(outer)
    def _():
        far_give().wait_recv()

    for c in range(pieces):
        column(spots - 1, c, last_chunk)
        if c == 0:
            pages_to_home()

    @pl.when(outer)
    def _():
        far_give().wait_send()
        for c in range(pieces):
            far_copy(c).wait_send()


    def drain_attn(b, carry):
        for g in range(blocks):
            attn_copy(b, g).wait_send()
        return carry

    lax.fori_loop(0, branches, drain_attn, 0)

    def drain_weight(step, carry):
        for c in range(pieces):
            to_mate(step, c).wait_send()
            for k in range(1, chips):
                to_chip(step, c, k).wait_send()
            for k in range(chips):
                to_core(step, c, k).wait_send()
        return carry

    lax.fori_loop(0, spots, drain_weight, 0)

    def drain_chunks(step, carry):
        def over(b, inner):
            for c in range(pieces):
                chunk_copy(step, b, c).wait_send()
            return inner

        return lax.fori_loop(0, branches, over, carry)

    lax.fori_loop(0, spots - 1, drain_chunks, 0)
    for k in range(1, chips):
        across(k).wait_send()
    for k in range(chips):
        beside(k).wait_send()
    for k in range(1, spots):
        to_row(k).wait_send()
    to_side.wait_send()
    for part in range(ratio):
        home_local(part).wait()
        for k in range(1, n_pre):
            to_home(k, part).wait_send()
            to_home(k, part).wait_recv()


def settle_kernel(*refs):
    count = (len(refs) - 1) // 2
    sem = refs[-1]
    copies = [
        pltpu.make_async_copy(refs[i], refs[count + i], sem.at[i]) for i in range(count)
    ]
    for copy in copies:
        copy.start()
    for copy in copies:
        copy.wait()


def settle(*arrays):
    anywhere = pl.BlockSpec(memory_space=pl.ANY)
    return pl.pallas_call(
        settle_kernel,
        out_shape=tuple(jax.ShapeDtypeStruct(a.shape, a.dtype) for a in arrays),
        in_specs=[anywhere] * len(arrays),
        out_specs=(anywhere,) * len(arrays),
        scratch_shapes=[pltpu.SemaphoreType.DMA((len(arrays),))],
        name="settle",
    )(*arrays)


def layer(lists, reach, owner, kv, pool, queries, own, weight, n_pre, n_dec):
    branches, page_len, depth = queries.shape
    count = pool.shape[0]
    cols = weight.shape[1] // n_dec
    ratio = n_dec // n_pre
    chips = n_pre // 2
    spots = n_dec // 2
    blocks = depth // (min(BLOCK, depth // (PAIR * HD)) * PAIR * HD)
    bf16 = jnp.bfloat16
    anywhere = pl.BlockSpec(memory_space=pl.ANY)
    dma = pltpu.SemaphoreType.DMA
    return pl.pallas_call(
        functools.partial(layer_kernel, n_pre, n_dec),
        out_shape=(
            pltpu.VMEM((branches, page_len, cols), bf16),
            pltpu.VMEM((n_pre, page_len, ratio * kv.shape[2]), bf16),
        ),
        in_specs=[anywhere] * 8,
        out_specs=(VMEM, VMEM),
        scratch_shapes=[
            pltpu.VMEM((count * n_pre,) + pool.shape[1:], bf16),
            pltpu.VMEM(queries.shape, bf16),
            pltpu.VMEM(own.shape, bf16),
            pltpu.VMEM((count * n_pre * page_len, 2 * HD), bf16),
            pltpu.VMEM((branches, page_len, 2 * depth), bf16),
            pltpu.VMEM((spots, 2 * depth, cols), bf16),
            pltpu.VMEM((spots, branches, page_len, cols), bf16),
            pltpu.VMEM((spots + 1, branches, page_len, cols), bf16),
            pltpu.VMEM((branches, 1, count * n_pre * page_len), jnp.float32),
            pltpu.VMEM((spots, 2) + kv.shape[1:], bf16),
            pltpu.VMEM((spots, 2) + kv.shape[1:], bf16),
            pltpu.VMEM((2, spots) + kv.shape[1:], bf16),
            pltpu.SMEM(lists.shape, jnp.int32),
            pltpu.SMEM(reach.shape, jnp.int32),
            pltpu.SMEM(owner.shape, jnp.int32),
            pltpu.VMEM(kv.shape, bf16),
            pltpu.VMEM((depth, cols), bf16),
            pltpu.VMEM((page_len, cols), bf16),
            pltpu.VMEM((page_len, cols), bf16),
            pltpu.VMEM((page_len, cols), bf16),
            dma((8,)),
            dma((spots,)),
            dma((n_pre,)),
            dma((n_pre,)),
            dma((spots,)),
            dma((spots,)),
            dma((1,)),
            dma((2,)),
            dma((n_pre, ratio)),
            dma((n_pre, ratio)),
            dma((branches, blocks)),
            dma((branches, blocks)),
            dma((spots, PIECES)),
            dma((spots, PIECES)),
            dma((spots, PIECES, chips)),
            dma((spots, PIECES, chips)),
            dma((spots, PIECES, chips)),
            dma((spots, PIECES, chips)),
            pltpu.SemaphoreType.REGULAR((2, spots - 2)),
            dma((spots, branches, PIECES)),
            dma((spots + 1, branches, PIECES)),
            dma((PIECES,)),
            dma((PIECES,)),
            dma((2,)),
        ],
        compiler_params=pltpu.CompilerParams(
            has_side_effects=True, collective_id=0, vmem_limit_bytes=62 * 2**20
        ),
        name="layer",
    )(lists, reach, owner, kv, pool, queries, own, weight)


def on_device(
    queries, branch_kv, pool_kv, page_lists, anc_len, dec_owner, output_projection_weight
):
    n_pre = lax.axis_size("pre")
    n_dec = lax.axis_size("dec")
    dec_idx = lax.axis_index("dec")
    kv_cols = pool_kv.shape[2]
    if kv_cols < 2 * HD:
        other_pool, other_own = from_partner((pool_kv, branch_kv), "dec", 0)
        first_half = dec_idx % 2 == 0
        pool = jnp.where(
            first_half,
            jnp.concatenate([pool_kv, other_pool], 2),
            jnp.concatenate([other_pool, pool_kv], 2),
        )
        own = jnp.where(
            first_half,
            jnp.concatenate([branch_kv, other_own], 2),
            jnp.concatenate([other_own, branch_kv], 2),
        )
    else:
        pool, own = pool_kv, branch_kv

    layer_out, decode_pages = layer(
        page_lists,
        anc_len,
        dec_owner,
        branch_kv,
        pool,
        queries,
        own,
        output_projection_weight,
        n_pre,
        n_dec,
    )
    return (layer_out, decode_pages)


def solution(mesh):
    in_specs = (
        P("pre", None, "dec"),
        P("pre", None, "dec"),
        P("pre", None, "dec"),
        P(),
        P(),
        P(),
        P("dec", None),
    )
    out_specs = (P("pre", None, "dec"), P("dec", None, "pre"))
    return jax.shard_map(
        on_device, mesh=mesh, in_specs=in_specs, out_specs=out_specs, check_vma=False
    )
```
